256 devices in a mesh: role: 2 (over core), grp: 4 (over x), seq: 32 (over z, y).
Axes of the slice: x: 4, y: 4, z: 8, core: 2. Of those that a mesh axis runs over, the one named last changes fastest.
Arguments:
- tokens: bfloat16 [8, 2048, 2048], P(('role', 'grp'), 'seq'), may hold values from -8 to 8
- parents: int32 [8, 64], P(('role', 'grp')), may hold values from 0 to 62, as said below
- route_ids: int32 [8, 2048, 8], P(('role', 'grp'), 'seq'), may hold values from 0 to 127, all different within a row; in each aligned block of 64 rows (0 to 63, 64 to 127, ..., all dimensions but the last counted through in order) at most 6 rows name the same one
- route_gates: float32 [8, 2048, 8], P(('role', 'grp'), 'seq'), may hold values from 0.02 to 0.25
- input_gain: float32 [2048], replicated, may hold values from 0.1 to 1.9
- q_gain: float32 [128], replicated, may hold values from 0.5 to 25
- k_gain: float32 [128], replicated, may hold values from 0.5 to 25
- post_gain: float32 [2048], replicated, may hold values from 0.1 to 1.9
- w_query: bfloat16 [2048, 4096], P(None, 'seq'), may hold values from -0.125 to 0.125
- w_keyval: bfloat16 [4, 2048, 256], replicated, may hold values from -0.125 to 0.125
- w_out: bfloat16 [4096, 2048], P('seq'), may hold values from -0.09375 to 0.09375
- w_gate_up: bfloat16 [128, 2, 2048, 768], P(('grp', 'seq'), None, None, 'role'), may hold values from -0.125 to 0.125
- w_down: bfloat16 [128, 768, 2048], P(('grp', 'seq'), 'role'), may hold values from -0.21875 to 0.21875
Outputs:
- layer_out: bfloat16 [8, 2048, 2048], P(('role', 'grp'), 'seq')
The draws below stay inside these ranges and needn't reach their ends.
Inputs may be any that keep to these rules, and one draw needn't show every extreme that they name: parents[s, 0] = 0; for a >= 1, parents[s, a] < a; the last node's parent is node 62. `route_ids`: each token names 8 different experts; among the 64 tokens of one device no expert is named more than 6 times, and in every draw some expert is named exactly 6 times by the tokens of some device.
All inputs are finite; a program needn't handle non-finite values.
Results may differ from the reference program's by a relative error of at most 0.018.
The reference program's roundings to bfloat16 on the way (of `normed`, `probs`, `attended`, `middle`, `post_normed`, `hidden` and `expert_out`) count: a program that leaves them out, or rounds other values in their place, can miss the bound.
Values may be sent and summed in bfloat16 or wider, within the bound.
No kernel may reach another device: no remote copies, remote signals or barrier semaphores. Data moves between devices by JAX's collectives and lax.ppermute only.
A program may use at most 128 MiB of HBM per device.

```python
import math
import jax
import jax.numpy as jnp
import numpy as np
from jax import lax

D = 2048
HEADS = 32
KV_HEADS = 4
HEAD_DIM = 128
EXP_FF = 768
TOPK = 8
NODE = 32
TOK_DEV = 64
EXPERTS = 128
LEN = 2048
SEQS = 8
NODES = 64
CAP = 6
N_ROLE = 2
N_GRP = 4
N_SEQ = 32


def draw_tokens(key, part):
    base_draw = jnp.clip(jax.random.normal(jax.random.fold_in(key, 11), (SEQS, LEN, D), jnp.float32), -5.0, 5.0)
    col_scale = jnp.exp(jax.random.uniform(jax.random.fold_in(key, 12), (D,), jnp.float32, math.log(0.3), math.log(3.0)))
    row_scale = jnp.exp(jax.random.uniform(jax.random.fold_in(key, 13), (SEQS, LEN, 1), jnp.float32, math.log(0.3), math.log(3.0)))
    values = 0.15 * base_draw * col_scale * row_scale
    return jnp.clip(values, -8.0, 8.0).astype(jnp.bfloat16)


def draw_parents(key, part):
    raw_bits = jax.random.randint(jax.random.fold_in(key, 21), (SEQS, NODES), 0, 1 << 20, dtype=jnp.int32)
    node_index = jnp.arange(NODES, dtype=jnp.int32)
    upper_bound = jnp.maximum(node_index, 1)
    drawn = (raw_bits % upper_bound[None, :]).astype(jnp.int32)
    last_parent = jnp.full((SEQS, NODES), max(NODES - 2, 0), jnp.int32)
    return jnp.where((node_index == NODES - 1)[None, :], last_parent, drawn).astype(jnp.int32)


def spiked_gain(key, salt):
    base_gain = jax.random.uniform(jax.random.fold_in(key, salt), (HEAD_DIM,), jnp.float32, 0.5, 1.5)
    return base_gain


def draw_q_gain(key, part):
    return spiked_gain(key, 31)


def draw_k_gain(key, part):
    return spiked_gain(key, 32)


def steps_of(stream_key, shape, shards, low, top_value):
    def one(axis_at, blocks):
        steps = jax.random.uniform(jax.random.fold_in(jax.random.fold_in(stream_key, 6), axis_at), (blocks,), jnp.float32, low / len(shards), top_value / len(shards))
        return jnp.repeat(jnp.exp(steps), shape[axis_at] // blocks).reshape((-1,) + (1,) * (len(shape) - axis_at - 1))

    factor_of = one(*shards[0])
    for cut in shards[1:]:
        factor_of = factor_of * one(*cut)
    return factor_of


def shared_out(rng, own, number, rows, amount, top, most, slope):
    ranking = jax.random.permutation(rng, amount)
    packed, usual = load_shares(amount, rows * top, most, slope, True), load_shares(amount, rows * top, most, slope, False)
    places = jnp.arange(amount)

    def named(lengths, offset_by):
        used = int((lengths > 0).sum())
        fixed = max(1, used // 4)
        passed = fixed + (places - fixed + offset_by * (used - fixed)) % max(1, amount - fixed)
        return jnp.zeros((amount,), jnp.int32).at[ranking[jnp.where(places < fixed, places, passed)]].set(jnp.asarray(lengths, jnp.int32))

    lengths = jnp.where(number % 4 == 0, named(packed, number // 4), named(usual, number - number // 4 - 1))
    mixed = jax.random.permutation(jax.random.fold_in(own, 3), amount)
    donor, sink = mixed[0:amount // 2 * 2:2], mixed[1:amount // 2 * 2:2]
    room = jnp.minimum(lengths[donor] - 1, most - lengths[sink]) // 2
    room = jnp.where((donor == ranking[0]) | (sink == ranking[0]) | (lengths[sink] == 0), 0, jnp.maximum(room, 0))
    passed = jax.random.randint(jax.random.fold_in(own, 4), (amount // 2,), 0, 1 << 20) % (room + 1)
    lengths = lengths.at[donor].add(-passed).at[sink].add(passed)
    members = jnp.searchsorted(jnp.cumsum(lengths), jnp.arange(rows * top), side="right").astype(jnp.int32)
    grid = members.reshape(top, rows).T
    grid = grid[jax.random.permutation(jax.random.fold_in(own, 1), rows)]
    offset_by = jax.random.randint(jax.random.fold_in(own, 2), (rows, 1), 0, top)
    return jnp.take_along_axis(grid, (jnp.arange(top)[None, :] + offset_by) % top, axis=1)


def load_shares(count, total, reach, skew, full):
    loads = [(1 << 20) // math.isqrt(rank ** skew) + 1 for rank in range(1, count + 1)]
    largest = reach if full else min(reach, max(-(-total // count), total * loads[0] // sum(loads)))
    least = 1 if total - largest >= count - 1 else 0
    counts, spare = [largest] + [least] * (count - 1), total - largest - least * (count - 1)
    while spare > 0:
        movable = [i for i in range(1, count) if counts[i] < largest] or [i for i in range(1, count) if counts[i] < reach]
        whole, left = sum([loads[i] for i in movable]), spare
        for i in movable:
            extra = min(reach - counts[i], max(1, left * loads[i] // whole), spare)
            counts[i] = counts[i] + extra
            spare = spare - extra
    return np.array(counts)


def scatter_about(stream_key, dims, deviation, reach, pieces=(), kind=jnp.bfloat16):
    loudness = steps_of(stream_key, dims, pieces, -0.22, 0.18) if pieces else 1.0
    array = jax.random.normal(stream_key, dims, jnp.float32) * deviation * loudness
    return jnp.minimum(jnp.maximum(array, -reach), reach).astype(kind)


def setup_inputs(seed: int = 0) -> dict:
    streams_of = jax.random.split(jax.random.key(seed), 14)
    tokens = draw_tokens(jax.random.fold_in(streams_of[13], 71), 0)
    parents = draw_parents(jax.random.fold_in(streams_of[13], 71), 0)
    route_ids_keys = jax.random.split(jax.random.fold_in(streams_of[2], 1), SEQS * LEN // TOK_DEV)
    route_ids_turns = jax.random.permutation(jax.random.fold_in(streams_of[2], 3), SEQS * LEN // TOK_DEV)
    route_ids = jax.vmap(lambda own, number: shared_out(jax.random.fold_in(streams_of[2], 2), own, number, TOK_DEV, EXPERTS, TOPK, CAP, 2))(route_ids_keys, route_ids_turns).reshape((SEQS, LEN, TOPK))
    route_gates = jnp.clip(0.02 + 0.23 * jax.random.uniform(streams_of[3], (SEQS, LEN, TOPK), jnp.float32) ** steps_of(streams_of[3], (SEQS, LEN, TOPK), ((0, 8), (1, 32)), -0.2, 0.2), 0.02, 0.25)
    input_gain = jnp.clip(1.0 + 0.18 * jax.random.normal(streams_of[4], (D,), jnp.float32), 0.1, 1.9)
    q_gain = draw_q_gain(jax.random.fold_in(streams_of[13], 71), 0)
    k_gain = draw_k_gain(jax.random.fold_in(streams_of[13], 71), 0)
    post_gain = jnp.clip(1.0 + 0.18 * jax.random.normal(streams_of[7], (D,), jnp.float32), 0.1, 1.9)
    w_query = scatter_about(streams_of[8], (D, HEADS * HEAD_DIM), D ** -0.5, 0.125, ((1, 32),))
    w_keyval = scatter_about(streams_of[9], (KV_HEADS, D, 2 * HEAD_DIM), D ** -0.5, 0.125)
    w_out = scatter_about(streams_of[10], (HEADS * HEAD_DIM, D), (HEADS * HEAD_DIM) ** -0.5, 0.09375, ((0, 32),))
    w_gate_up = scatter_about(streams_of[11], (EXPERTS, 2, D, EXP_FF), D ** -0.5, 0.125, ((0, 128), (3, 2)))
    w_down = scatter_about(streams_of[12], (EXPERTS, EXP_FF, D), EXP_FF ** -0.5, 0.21875, ((0, 128), (1, 2)))
    return dict(tokens=tokens, parents=parents, route_ids=route_ids, route_gates=route_gates, input_gain=input_gain, q_gain=q_gain, k_gain=k_gain, post_gain=post_gain, w_query=w_query, w_keyval=w_keyval, w_out=w_out, w_gate_up=w_gate_up, w_down=w_down)


EPSILON = 1e-06
ROPE_BASE = 1000000.0
HIGHEST = lax.Precision.HIGHEST
MASKED = -1e+30

def rms_scale(values, gain):
    mean_sq = lax.optimization_barrier(jnp.mean(values * values, axis=-1, keepdims=True))
    return values * lax.rsqrt(mean_sq + EPSILON) * gain

def ancestry(parent_row, node_count):
    node_ids = jnp.arange(node_count, dtype=jnp.int32)
    parent_hot = (parent_row.astype(jnp.int32)[:, None] == node_ids[None, :]).astype(jnp.float32)
    reach_table = jnp.maximum(parent_hot, jnp.eye(node_count, dtype=jnp.float32))
    for repeat_index in range(node_count.bit_length()):
        reach_table = (jnp.dot(reach_table, reach_table, precision=HIGHEST) > 0.5).astype(jnp.float32)
    return reach_table

def token_positions(parent_row, length):
    reach_table = ancestry(parent_row, length // NODE)
    depth = lax.optimization_barrier(jnp.sum(reach_table, axis=1)) - 1.0
    offsets = (jnp.arange(length, dtype=jnp.int32) % NODE).astype(jnp.float32)
    return (reach_table, jnp.repeat(depth, NODE) * NODE + offsets)

def rotate(values, positions):
    half_dim = values.shape[-1] // 2
    frequency = jnp.power(ROPE_BASE, -2.0 * jnp.arange(half_dim, dtype=jnp.float32) / values.shape[-1])
    angles = positions[:, None] * frequency[None, :]
    cosine = jnp.cos(angles)[:, None, :]
    sines = jnp.sin(angles)[:, None, :]
    first_half = values[..., :half_dim]
    second = values[..., half_dim:]
    return jnp.concatenate([first_half * cosine - second * sines, second * cosine + first_half * sines], axis=-1)

def reference(tokens, parents, route_ids, route_gates, input_gain, q_gain, k_gain, post_gain, w_query, w_keyval, w_out, w_gate_up, w_down):
    seq_total, length, model_width = tokens.shape
    residual = tokens.astype(jnp.float32)
    normed = rms_scale(residual, input_gain).astype(jnp.bfloat16)
    heads_per_kv = HEADS // KV_HEADS
    keyval_weight = jnp.transpose(w_keyval, (1, 0, 2)).reshape(model_width, KV_HEADS * 2 * HEAD_DIM)
    inv_scale = 1.0 / math.sqrt(HEAD_DIM)

    def one_sequence(operands):
        rows_in, parent_row = operands
        queries = jnp.dot(rows_in, w_query, preferred_element_type=jnp.float32).astype(jnp.bfloat16)
        keyval = jnp.dot(rows_in, keyval_weight, preferred_element_type=jnp.float32).astype(jnp.bfloat16)
        keyval = keyval.reshape(length, KV_HEADS, 2 * HEAD_DIM)
        reach_table, positions = token_positions(parent_row, length)
        q_rot = rotate(rms_scale(queries.astype(jnp.float32).reshape(length, HEADS, HEAD_DIM), q_gain), positions).astype(jnp.bfloat16)
        k_rot = rotate(rms_scale(keyval[..., :HEAD_DIM].astype(jnp.float32), k_gain), positions).astype(jnp.bfloat16)
        values_in = keyval[..., HEAD_DIM:]
        k_heads = jnp.repeat(k_rot, heads_per_kv, axis=1)
        v_heads = jnp.repeat(values_in, heads_per_kv, axis=1)
        scores = jnp.einsum('qhd,khd->hqk', q_rot.astype(jnp.float32), k_heads.astype(jnp.float32)) * inv_scale
        token_ids = jnp.arange(length, dtype=jnp.int32)
        ancestors = jnp.repeat(jnp.repeat(reach_table, NODE, axis=0), NODE, axis=1) > 0.5
        seen = ancestors & (token_ids[None, :] <= token_ids[:, None])
        scores = jnp.where(seen[None], scores, MASKED)
        row_max = lax.optimization_barrier(jnp.max(scores, axis=-1, keepdims=True))
        exp_scores = jnp.exp(scores - row_max)
        probs = (exp_scores / lax.optimization_barrier(jnp.sum(exp_scores, axis=-1, keepdims=True))).astype(jnp.bfloat16)
        attended = jnp.einsum('hqk,khd->qhd', probs.astype(jnp.float32), v_heads.astype(jnp.float32))
        attended = attended.astype(jnp.bfloat16).reshape(length, HEADS * HEAD_DIM)
        return jnp.dot(attended, w_out, preferred_element_type=jnp.float32)
    attn_out = lax.map(one_sequence, (normed, parents))
    middle = lax.optimization_barrier((residual + attn_out).astype(jnp.bfloat16))
    middle_f = middle.astype(jnp.float32).reshape(-1, model_width)
    post_normed = rms_scale(middle_f, post_gain).astype(jnp.bfloat16)
    expert_ids = route_ids.reshape(-1).astype(jnp.int32)
    gate_flat = route_gates.reshape(-1)
    limit = N_ROLE * N_GRP * N_SEQ * CAP

    def add_expert(moe_sum, expert_index):
        chosen = expert_ids == expert_index
        found = jnp.nonzero(chosen, size=limit, fill_value=0)[0].astype(jnp.int32)
        live = (jnp.arange(limit, dtype=jnp.int32) < jnp.sum(chosen.astype(jnp.int32))).astype(jnp.float32)
        token_index = found // TOPK
        inputs = post_normed[token_index]
        gate_proj = jnp.dot(inputs, w_gate_up[expert_index, 0], preferred_element_type=jnp.float32)
        up_proj = jnp.dot(inputs, w_gate_up[expert_index, 1], preferred_element_type=jnp.float32)
        hidden = (jax.nn.silu(gate_proj) * up_proj).astype(jnp.bfloat16)
        expert_out = jnp.dot(hidden, w_down[expert_index], preferred_element_type=jnp.float32).astype(jnp.bfloat16)
        scaled = (gate_flat[found] * live)[:, None] * expert_out.astype(jnp.float32)
        return (moe_sum.at[token_index].add(scaled), None)
    moe_sum = lax.scan(add_expert, jnp.zeros(middle_f.shape, jnp.float32), jnp.arange(EXPERTS, dtype=jnp.int32))[0]
    return (middle_f + moe_sum).astype(jnp.bfloat16).reshape(tokens.shape)
```

```python
import functools
import math

import jax
import jax.numpy as jnp
from jax import lax
from jax.experimental import pallas as pl
from jax.experimental.pallas import tpu as pltpu
from jax.sharding import Mesh, PartitionSpec as P

NODE = 32
CAP = 6
EPSILON = 1e-06
ROPE_BASE = 1000000.0
MASKED = -1e30
BF16 = jnp.bfloat16
F32 = jnp.float32
N_Z = 8
N_Y = 4
N_X = 4
VMEM_LIMIT = 60 * 1024 * 1024


def shift(x, axis, size, by):
    return lax.ppermute(x, axis, [(i, (i + by) % size) for i in range(size)])


def ring_gather(x):
    half = x.shape[0] // 2
    fwd, bwd = [x], [x]
    for _ in range(3):
        fwd.append(shift(fwd[-1], "z", N_Z, 1))
        bwd.append(shift(bwd[-1], "z", N_Z, N_Z - 1))
    far_a = shift(fwd[3][:half], "z", N_Z, 1)
    far_b = shift(bwd[3][half:], "z", N_Z, N_Z - 1)
    return jnp.concatenate(fwd + [far_a, far_b] + bwd[:0:-1], axis=0)


def ring_scatter(slabs):
    half = slabs.shape[1] // 2

    def plus(a, b):
        return (a.astype(F32) + b.astype(F32)).astype(BF16)

    far_a = shift(slabs[4, :half], "z", N_Z, 1)
    far_b = shift(slabs[4, half:], "z", N_Z, N_Z - 1)
    fwd = jnp.concatenate([plus(slabs[5, :half], far_a), slabs[5, half:]], axis=0)
    bwd = jnp.concatenate([slabs[3, :half], plus(slabs[3, half:], far_b)], axis=0)
    for step in (1, 2, 3):
        fwd = shift(fwd, "z", N_Z, 1)
        bwd = shift(bwd, "z", N_Z, N_Z - 1)
        if step < 3:
            fwd = plus(fwd, slabs[5 + step])
            bwd = plus(bwd, slabs[3 - step])
    return fwd.astype(F32) + bwd.astype(F32) + slabs[0].astype(F32)


def rms_scale(values, gain):
    mean_sq = jnp.mean(values * values, axis=-1, keepdims=True)
    return values * lax.rsqrt(mean_sq + EPSILON) * gain


def qkv_kernel(kv_ref, xa, xb, gain, wq0, wq1, wq2, wq3, wkv, cosd, sind, qg, kg, q_out, kv_out, w_scr):
    @pl.when(pl.program_id(0) == 0)
    def _():
        for h, w in enumerate((wq0, wq1, wq2, wq3)):
            w_scr[:, h * 128 : (h + 1) * 128] = w[...]
        w_scr[:, 512:768] = wkv[0]

    width = xa.shape[1]
    fa = xa[...].astype(F32)
    fb = xb[...].astype(F32)
    mean_sq = (
        jnp.sum(fa * fa, axis=-1, keepdims=True) + jnp.sum(fb * fb, axis=-1, keepdims=True)
    ) / (2 * width)
    scale = lax.rsqrt(mean_sq + EPSILON)
    na = (fa * scale * gain[:, :width]).astype(BF16)
    nb = (fb * scale * gain[:, width:]).astype(BF16)
    proj = jnp.dot(na, w_scr[:width], preferred_element_type=F32) + jnp.dot(
        nb, w_scr[width:], preferred_element_type=F32
    )
    proj = proj.astype(BF16)
    cos = cosd[...]
    sin = sind[...]

    def turned(part, g):
        u = rms_scale(part.astype(F32), g[...])
        return (u * cos + pltpu.roll(u, 64, 1) * sin).astype(BF16)

    for h in range(4):
        q_out[h] = turned(proj[:, h * 128 : (h + 1) * 128], qg)
    kv_out[:, :128] = turned(proj[:, 512:640], kg)
    kv_out[:, 128:] = proj[:, 640:768]


def qkv(kv_index, xa, xb, gain, wq, w_keyval, cosd, sind, q_gain, k_gain):
    rows = 256
    total = xa.shape[0]
    whole = lambda shape: pl.BlockSpec(shape, lambda i, s: (0,) * len(shape))
    return pl.pallas_call(
        qkv_kernel,
        out_shape=(
            jax.ShapeDtypeStruct((4, total, 128), BF16),
            jax.ShapeDtypeStruct((total, 256), BF16),
        ),
        grid_spec=pltpu.PrefetchScalarGridSpec(
            num_scalar_prefetch=1,
            grid=(total // rows,),
            in_specs=[
                pl.BlockSpec((rows, 1024), lambda i, s: (i, 0)),
                pl.BlockSpec((rows, 1024), lambda i, s: (i, 0)),
                whole((1, 2048)),
                whole((2048, 128)),
                whole((2048, 128)),
                whole((2048, 128)),
                whole((2048, 128)),
                pl.BlockSpec((1, 2048, 256), lambda i, s: (s[0], 0, 0)),
                pl.BlockSpec((rows, 128), lambda i, s: (i, 0)),
                pl.BlockSpec((rows, 128), lambda i, s: (i, 0)),
                whole((1, 128)),
                whole((1, 128)),
            ],
            out_specs=(
                pl.BlockSpec((4, rows, 128), lambda i, s: (0, i, 0)),
                pl.BlockSpec((rows, 256), lambda i, s: (i, 0)),
            ),
            scratch_shapes=[pltpu.VMEM((2048, 768), BF16)],
        ),
        compiler_params=pltpu.CompilerParams(vmem_limit_bytes=VMEM_LIMIT),
        name="qkv",
    )(kv_index, xa, xb, gain, *wq, w_keyval, cosd, sind, q_gain, k_gain)


def attend_kernel(place, q, kv, bias, wo0, wo1, wo2, wo3, out, att, w_scr):
    k = pl.program_id(0)
    z = place[0]
    y = place[1]
    q_plane = lax.rem(z - k + N_Z, N_Z)

    @pl.when(k == 0)
    def _():
        for h, w in enumerate((wo0, wo1, wo2, wo3)):
            w_scr[h * 128 : (h + 1) * 128] = w[...]

    queries = q[...].reshape(256, 128)
    inv_scale = 1.0 / math.sqrt(128)
    row = lax.broadcasted_iota(jnp.int32, (64, 256), 0)
    col = lax.broadcasted_iota(jnp.int32, (64, 256), 1)
    later = (col // 64 == y) & (col % 64 > row)

    def scores_of(plane):
        j = lax.rem(z - plane + N_Z, N_Z)
        rows = pl.ds(pl.multiple_of(j * 64, 64), 64)
        keys = kv[:, rows, :128].reshape(256, 128)
        values = kv[:, rows, 128:].reshape(256, 128)
        cols = pl.ds(pl.multiple_of(j * 256, 256), 256)
        mask = jnp.where(row < 32, bias[0, 0:1, cols], bias[0, 1:2, cols])
        scores = (
            lax.dot_general(queries, keys, (((1,), (1,)), ((), ())), preferred_element_type=F32)
            * inv_scale
        )
        return scores.reshape(4, 64, 256), mask, values

    def fold(scores, values, top, total, mixed):
        new_top = jnp.maximum(top, jnp.max(scores, axis=-1, keepdims=True))
        old = jnp.exp(top - new_top)
        probs = jnp.exp(scores - new_top)
        total = old * total + jnp.sum(probs, axis=-1, keepdims=True)
        mixed = old * mixed + jnp.dot(probs.astype(BF16), values, preferred_element_type=F32)
        return new_top, total, mixed

    scores, mask, values = scores_of(q_plane)
    hidden = (mask < 0.5) | later
    scores = jnp.where(hidden[None], MASKED, scores).reshape(256, 256)
    top = jnp.max(scores, axis=-1, keepdims=True)
    probs = jnp.exp(scores - top)
    total = jnp.sum(probs, axis=-1, keepdims=True)
    mixed = jnp.dot(probs.astype(BF16), values, preferred_element_type=F32)

    def step(plane, carry):
        scores, mask, values = scores_of(plane)
        scores = jnp.where((mask < 0.5)[None], MASKED, scores).reshape(256, 256)
        return fold(scores, values, *carry)

    top, total, mixed = lax.fori_loop(0, q_plane, step, (top, total, mixed))
    attended = (mixed / total).astype(BF16)
    for h in range(4):
        att[pl.ds(pl.multiple_of(k * 64, 64), 64), h * 128 : (h + 1) * 128] = attended[
            h * 64 : (h + 1) * 64
        ]

    @pl.when(k == N_Z - 1)
    def _():
        out[...] = jnp.dot(att[...], w_scr[...], preferred_element_type=F32).astype(BF16)


def attend(place, q, kv, bias, wo):
    whole = lambda shape: pl.BlockSpec(shape, lambda i, s: (0,) * len(shape))
    return pl.pallas_call(
        attend_kernel,
        out_shape=jax.ShapeDtypeStruct((512, 2048), BF16),
        grid_spec=pltpu.PrefetchScalarGridSpec(
            num_scalar_prefetch=1,
            grid=(N_Z,),
            in_specs=[
                pl.BlockSpec((4, 64, 128), lambda i, s: (0, i, 0)),
                whole((N_Y, 512, 256)),
                pl.BlockSpec((1, 2, 2048), lambda i, s: (i, 0, 0)),
                whole((128, 2048)),
                whole((128, 2048)),
                whole((128, 2048)),
                whole((128, 2048)),
            ],
            out_specs=whole((512, 2048)),
            scratch_shapes=[pltpu.VMEM((512, 512), BF16), pltpu.VMEM((512, 2048), BF16)],
        ),
        compiler_params=pltpu.CompilerParams(vmem_limit_bytes=VMEM_LIMIT),
        name="attend",
    )(place, q, kv, bias, *wo)


def route_kernel(place, meta, spread_out, gate_a, gate_b):
    slots = spread_out.shape[0]
    rows = meta.shape[0]
    per = slots // 16
    z = place[0]
    info = meta[...].astype(F32)
    member = lax.broadcasted_iota(jnp.int32, (1, 128), 1)
    expert = (member // N_Y) * (N_Z * N_Y) + z * N_Y + member % N_Y
    expert = jnp.where(member < 16, expert, -1).astype(F32)
    hot = jnp.zeros((rows, 128), F32)
    high = jnp.zeros((rows, 128), F32)
    low = jnp.zeros((rows, 128), F32)
    for i in range(8):
        same = info[:, i : i + 1] == expert
        hot = hot + jnp.where(same, 1.0, 0.0)
        high = high + jnp.where(same, info[:, 8 + i : 9 + i], 0.0)
        low = low + jnp.where(same, info[:, 16 + i : 17 + i], 0.0)
    upto = lax.broadcasted_iota(jnp.int32, (rows, rows), 0) >= lax.broadcasted_iota(
        jnp.int32, (rows, rows), 1
    )
    count = jnp.dot(
        jnp.where(upto, 1.0, 0.0).astype(BF16), hot.astype(BF16), preferred_element_type=F32
    )
    rank = (count * hot).astype(BF16)
    slot_of = lax.broadcasted_iota(jnp.int32, (128, slots), 1) // per
    grow = jnp.where(
        slot_of == lax.broadcasted_iota(jnp.int32, (128, slots), 0), 1.0, 0.0
    ).astype(BF16)
    wide = jnp.dot(rank, grow, preferred_element_type=F32)
    nth = (lax.broadcasted_iota(jnp.int32, (1, slots), 1) % per + 1).astype(F32)
    at = wide == nth
    gate_a[...] = jnp.where(
        at, jnp.dot(high.astype(BF16), grow, preferred_element_type=F32), 0.0
    ).astype(BF16)
    gate_b[...] = jnp.where(
        at, jnp.dot(low.astype(BF16), grow, preferred_element_type=F32), 0.0
    ).astype(BF16)
    spread_out[...] = jnp.where(at, 1.0, 0.0).T.astype(BF16)


def route(place, meta, slots):
    rows = meta.shape[0]
    whole = lambda shape: pl.BlockSpec(shape, lambda i, s: (0,) * len(shape))
    return pl.pallas_call(
        route_kernel,
        out_shape=(
            jax.ShapeDtypeStruct((slots, rows), BF16),
            jax.ShapeDtypeStruct((rows, slots), BF16),
            jax.ShapeDtypeStruct((rows, slots), BF16),
        ),
        grid_spec=pltpu.PrefetchScalarGridSpec(
            num_scalar_prefetch=1,
            grid=(1,),
            in_specs=[whole(meta.shape)],
            out_specs=(whole((slots, rows)), whole((rows, slots)), whole((rows, slots))),
        ),
        compiler_params=pltpu.CompilerParams(vmem_limit_bytes=VMEM_LIMIT),
        name="route",
    )(place, meta)


def ffn_kernel(x, gu_a, gu_b, d_a, d_b, out):
    rows = x[...]

    def hidden(gu):
        gate = jnp.dot(rows, gu[0], preferred_element_type=F32)
        up = jnp.dot(rows, gu[1], preferred_element_type=F32)
        return (gate / (1.0 + jnp.exp(-gate)) * up).astype(BF16)

    out[...] = (
        jnp.dot(hidden(gu_a), d_a[...], preferred_element_type=F32)
        + jnp.dot(hidden(gu_b), d_b[...], preferred_element_type=F32)
    ).astype(BF16)


def ffn(x, gu_a, gu_b, d_a, d_b):
    rows = 256
    whole = lambda shape: pl.BlockSpec(
        shape, lambda i: (0,) * len(shape), pipeline_mode=pl.Buffered(1)
    )
    return pl.pallas_call(
        ffn_kernel,
        out_shape=jax.ShapeDtypeStruct(x.shape, BF16),
        grid=(x.shape[0] // rows,),
        in_specs=[
            pl.BlockSpec((rows, 2048), lambda i: (i, 0)),
            whole(gu_a.shape),
            whole(gu_b.shape),
            whole(d_a.shape),
            whole(d_b.shape),
        ],
        out_specs=pl.BlockSpec((rows, 2048), lambda i: (i, 0)),
        compiler_params=pltpu.CompilerParams(vmem_limit_bytes=VMEM_LIMIT),
        name="ffn",
    )(x, gu_a, gu_b, d_a, d_b)


def combine_kernel(ga, gb, r, out):
    rows = r[...]
    out[...] = (
        jnp.dot(ga[...], rows, preferred_element_type=F32)
        + jnp.dot(gb[...], rows, preferred_element_type=F32)
    ).astype(BF16)


def combine(ga, gb, r):
    cols = 512
    whole = lambda shape: pl.BlockSpec(shape, lambda i: (0,) * len(shape))
    return pl.pallas_call(
        combine_kernel,
        out_shape=jax.ShapeDtypeStruct((ga.shape[0], r.shape[1]), BF16),
        grid=(r.shape[1] // cols,),
        in_specs=[
            whole(ga.shape),
            whole(gb.shape),
            pl.BlockSpec((r.shape[0], cols), lambda i: (0, i)),
        ],
        out_specs=pl.BlockSpec((ga.shape[0], cols), lambda i: (0, i)),
        compiler_params=pltpu.CompilerParams(vmem_limit_bytes=VMEM_LIMIT),
        name="combine",
    )(ga, gb, r)


def ancestry(parent_row):
    nodes = parent_row.shape[0]
    ids = jnp.arange(nodes, dtype=jnp.int32)
    reach = ((parent_row[:, None] == ids[None, :]) | (ids[:, None] == ids[None, :])).astype(BF16)
    for _ in range((nodes - 1).bit_length()):
        reach = (jnp.dot(reach, reach, preferred_element_type=F32) > 0.5).astype(BF16)
    return reach


def body(
    tokens,
    parents,
    route_ids,
    route_gates,
    input_gain,
    q_gain,
    k_gain,
    post_gain,
    w_query,
    w_keyval,
    w_out,
    w_gate_up,
    w_down,
):
    z = lax.axis_index("z")
    y = lax.axis_index("y")
    place = jnp.stack([z, y]).astype(jnp.int32)
    half = 1024

    gates = route_gates[0]
    high = gates.astype(BF16)
    low = (gates - high.astype(F32)).astype(BF16)
    meta = jnp.concatenate(
        [route_ids[0].astype(BF16), high, low, jnp.zeros((64, 104), BF16)], axis=1
    )
    own = tokens[0]
    xa = ring_gather(own[:, :half])
    xb = ring_gather(jnp.concatenate([own[:, half:], meta], axis=1))
    wq = [w_query] + [shift(w_query, "y", N_Y, k) for k in (1, 3, 2)]
    meta_col = xb[:, half:]

    reach = ancestry(parents[0])
    depth = jnp.sum(reach.astype(F32), axis=1) - 1.0
    node_ids = jnp.arange(64, dtype=jnp.int32)
    t512 = jnp.arange(512, dtype=jnp.int32)
    node_of = ((z - t512 // 64) % N_Z) * 8 + y * 2 + (t512 % 64) // NODE
    depth_of = jnp.sum(
        jnp.where(node_of[:, None] == node_ids[None, :], depth[None, :], 0.0), axis=1
    )
    positions = depth_of * NODE + (t512 % NODE).astype(F32)
    frequency = jnp.power(ROPE_BASE, -2.0 * jnp.arange(64, dtype=F32) / 128)
    angles = positions[:, None] * frequency[None, :]
    cosine = jnp.cos(angles)
    sine = jnp.sin(angles)
    cosd = jnp.concatenate([cosine, cosine], axis=1)
    sind = jnp.concatenate([-sine, sine], axis=1)
    t16 = jnp.arange(16, dtype=jnp.int32)
    q_node = ((z - t16 // 2) % N_Z) * 8 + y * 2 + t16 % 2
    cols = jnp.arange(2048, dtype=jnp.int32)
    k_node = ((z - cols // 256) % N_Z) * 8 + (cols % 256) // NODE
    q_hot = (q_node[:, None] == node_ids[None, :]).astype(BF16)
    k_hot = (node_ids[:, None] == k_node[None, :]).astype(BF16)
    q_reach = jnp.dot(q_hot, reach, preferred_element_type=F32).astype(BF16)
    seen = jnp.dot(q_reach, k_hot, preferred_element_type=F32).reshape(8, 2, 2048)

    q, kv = qkv(
        (z // 2).reshape(1).astype(jnp.int32),
        xa,
        xb,
        input_gain.reshape(1, -1),
        wq,
        w_keyval,
        cosd,
        sind,
        q_gain.reshape(1, -1),
        k_gain.reshape(1, -1),
    )
    kv_all = lax.all_to_all(
        jnp.broadcast_to(kv[None], (N_Y,) + kv.shape), "y", 0, 0, tiled=True
    )
    wo = [w_out] + [shift(w_out, "y", N_Y, k) for k in (1, 3, 2)]
    swap = [(0, 1), (1, 0)]
    gate_up = w_gate_up[0]
    down = w_down[0]
    gate_up_b = lax.ppermute(gate_up, "role", swap)
    down_b = lax.ppermute(down, "role", swap)
    partial = attend(place, q, kv_all, seen, wo).reshape(8, 64, 2048)
    attn = jnp.concatenate(
        [ring_scatter(partial[:, :, :half]), ring_scatter(partial[:, :, half:])], axis=1
    )
    middle = (own.astype(F32) + attn).astype(BF16)
    middle_f = middle.astype(F32)
    post_normed = rms_scale(middle_f, post_gain).astype(BF16)

    slots = 16 * CAP * N_Z
    spread, gate_a, gate_b = route(place, meta_col, slots)
    pa = ring_gather(post_normed[:, :half])
    pb = ring_gather(post_normed[:, half:])
    outgoing = jnp.dot(
        spread, jnp.concatenate([pa, pb], axis=1), preferred_element_type=F32
    ).astype(BF16)
    received = lax.all_to_all(
        outgoing.reshape(16, CAP * N_Z, 2048), ("grp", "y"), 0, 0, tiled=True
    )
    result = ffn(received.reshape(slots, 2048), gate_up, gate_up_b, down, down_b)
    returned = lax.all_to_all(
        result.reshape(16, CAP * N_Z, 2048), ("grp", "y"), 0, 0, tiled=True
    )
    moe_part = combine(gate_a, gate_b, returned.reshape(slots, 2048)).reshape(8, 64, 2048)
    moe = jnp.concatenate(
        [ring_scatter(moe_part[:, :, :half]), ring_scatter(moe_part[:, :, half:])], axis=1
    )
    return (middle_f + moe).astype(BF16)[None]


def solution(mesh):
    split = Mesh(mesh.devices.reshape(2, 4, 8, 4), ("role", "grp", "z", "y"))
    seq = ("z", "y")
    in_specs = (
        P(("role", "grp"), seq, None),
        P(("role", "grp"), None),
        P(("role", "grp"), seq, None),
        P(("role", "grp"), seq, None),
        P(),
        P(),
        P(),
        P(),
        P(None, seq),
        P(),
        P(seq, None),
        P(("grp", "z", "y"), None, None, "role"),
        P(("grp", "z", "y"), "role", None),
    )
    out_specs = P(("role", "grp"), seq, None)
    return jax.shard_map(body, mesh=split, in_specs=in_specs, out_specs=out_specs, check_vma=False)
```

```python
import functools
import math

import jax
import jax.numpy as jnp
from jax import lax
from jax.experimental import pallas as pl
from jax.experimental.pallas import tpu as pltpu
from jax.sharding import Mesh, PartitionSpec as P

NODE = 32
CAP = 6
EPSILON = 1e-06
ROPE_BASE = 1000000.0
MASKED = -1e30
BF16 = jnp.bfloat16
F32 = jnp.float32
N_Z = 8
N_Y = 4
N_X = 4
VMEM_LIMIT = 60 * 1024 * 1024


def shift(x, axis, size, by):
    return lax.ppermute(x, axis, [(i, (i + by) % size) for i in range(size)])


def ring_gather(x, beside=None):
    half = x.shape[0] // 2
    fwd, bwd = [x], [x]
    for i in range(3):
        if i == 2 and beside is not None:
            fwd[2], beside = lax.optimization_barrier((fwd[2], beside))
        fwd.append(shift(fwd[-1], "z", N_Z, 1))
        bwd.append(shift(bwd[-1], "z", N_Z, N_Z - 1))
    far_a = shift(fwd[3][:half], "z", N_Z, 1)
    far_b = shift(bwd[3][half:], "z", N_Z, N_Z - 1)
    full = jnp.concatenate(fwd + [far_a, far_b] + bwd[:0:-1], axis=0)
    return full if beside is None else (full, beside)


def ring_scatter(slabs):
    half = slabs.shape[1] // 2

    def plus(a, b):
        return (a.astype(F32) + b.astype(F32)).astype(BF16)

    far_a = shift(slabs[4, :half], "z", N_Z, 1)
    far_b = shift(slabs[4, half:], "z", N_Z, N_Z - 1)
    fwd = jnp.concatenate([plus(slabs[5, :half], far_a), slabs[5, half:]], axis=0)
    bwd = jnp.concatenate([slabs[3, :half], plus(slabs[3, half:], far_b)], axis=0)
    for step in (1, 2, 3):
        fwd = shift(fwd, "z", N_Z, 1)
        bwd = shift(bwd, "z", N_Z, N_Z - 1)
        if step < 3:
            fwd = plus(fwd, slabs[5 + step])
            bwd = plus(bwd, slabs[3 - step])
    return fwd.astype(F32) + bwd.astype(F32) + slabs[0].astype(F32)


def rms_scale(values, gain):
    mean_sq = jnp.mean(values * values, axis=-1, keepdims=True)
    return values * lax.rsqrt(mean_sq + EPSILON) * gain


def kv_kernel(kv_ref, xa, xb, gain, wkv, cosd, sind, kg, kv_out, n_out):
    width = xa.shape[1]
    fa = xa[...].astype(F32)
    fb = xb[...].astype(F32)
    mean_sq = (
        jnp.sum(fa * fa, axis=-1, keepdims=True) + jnp.sum(fb * fb, axis=-1, keepdims=True)
    ) / (2 * width)
    scale = lax.rsqrt(mean_sq + EPSILON)
    na = (fa * scale * gain[:, :width]).astype(BF16)
    nb = (fb * scale * gain[:, width:]).astype(BF16)
    n_out[:, :width] = na
    n_out[:, width:] = nb
    proj = jnp.dot(na, wkv[0, :width], preferred_element_type=F32) + jnp.dot(
        nb, wkv[0, width:], preferred_element_type=F32
    )
    proj = proj.astype(BF16)
    u = rms_scale(proj[:, :128].astype(F32), kg[...])
    keys = (u * cosd[...] + pltpu.roll(u, 64, 1) * sind[...]).astype(BF16)
    for copy in range(N_Y):
        kv_out[copy, :, :128] = keys
        kv_out[copy, :, 128:] = proj[:, 128:]


def project_kv(kv_index, xa, xb, gain, w_keyval, cosd, sind, k_gain):
    rows = 256
    total = xa.shape[0]
    whole = lambda shape: pl.BlockSpec(shape, lambda i, s: (0,) * len(shape))
    return pl.pallas_call(
        kv_kernel,
        out_shape=(
            jax.ShapeDtypeStruct((N_Y, total, 256), BF16),
            jax.ShapeDtypeStruct((total, 2048), BF16),
        ),
        grid_spec=pltpu.PrefetchScalarGridSpec(
            num_scalar_prefetch=1,
            grid=(total // rows,),
            in_specs=[
                pl.BlockSpec((rows, 1024), lambda i, s: (i, 0)),
                pl.BlockSpec((rows, 1024), lambda i, s: (i, 0)),
                whole((1, 2048)),
                pl.BlockSpec((1, 2048, 256), lambda i, s: (s[0], 0, 0)),
                pl.BlockSpec((rows, 128), lambda i, s: (i, 0)),
                pl.BlockSpec((rows, 128), lambda i, s: (i, 0)),
                whole((1, 128)),
            ],
            out_specs=(
                pl.BlockSpec((N_Y, rows, 256), lambda i, s: (0, i, 0)),
                pl.BlockSpec((rows, 2048), lambda i, s: (i, 0)),
            ),
        ),
        compiler_params=pltpu.CompilerParams(vmem_limit_bytes=VMEM_LIMIT),
        name="project_kv",
    )(kv_index, xa, xb, gain, w_keyval, cosd, sind, k_gain)


def q_kernel(n, wq_own, wq_rest, cosd, sind, qg, q_out, w_scr):
    @pl.when(pl.program_id(0) == 0)
    def _():
        w_scr[:128] = wq_own[...]
        w_scr[128:] = wq_rest[...]

    proj = lax.dot_general(
        n[...], w_scr[...], (((1,), (1,)), ((), ())), preferred_element_type=F32
    ).astype(BF16)
    cos = cosd[...]
    sin = sind[...]
    for h in range(4):
        u = rms_scale(proj[:, h * 128 : (h + 1) * 128].astype(F32), qg[...])
        q_out[h] = (u * cos + pltpu.roll(u, 64, 1) * sin).astype(BF16)


def project_q(n, wq_own, wq_rest, cosd, sind, q_gain):
    rows = 256
    total = n.shape[0]
    whole = lambda shape: pl.BlockSpec(shape, lambda i: (0,) * len(shape))
    return pl.pallas_call(
        q_kernel,
        out_shape=jax.ShapeDtypeStruct((4, total, 128), BF16),
        grid=(total // rows,),
        in_specs=[
            pl.BlockSpec((rows, 2048), lambda i: (i, 0)),
            whole((128, 2048)),
            whole((384, 2048)),
            pl.BlockSpec((rows, 128), lambda i: (i, 0)),
            pl.BlockSpec((rows, 128), lambda i: (i, 0)),
            whole((1, 128)),
        ],
        out_specs=pl.BlockSpec((4, rows, 128), lambda i: (0, i, 0)),
        scratch_shapes=[pltpu.VMEM((512, 2048), BF16)],
        compiler_params=pltpu.CompilerParams(vmem_limit_bytes=VMEM_LIMIT),
        name="project_q",
    )(n, wq_own, wq_rest, cosd, sind, q_gain)


def attend_kernel(table, q, kv, seen, wo_own, wo_rest, out, att, w_scr, kv_scr):
    k = pl.program_id(0)
    z = table[0]
    base = 8 + k * 72

    @pl.when(k == 0)
    def _():
        w_scr[:128] = wo_own[...]
        w_scr[128:] = wo_rest[...]

    queries = q[...].reshape(256, 128)
    inv_scale = 1.0 / math.sqrt(128)
    row = lax.broadcasted_iota(jnp.int32, (64, 256), 0)
    col = lax.broadcasted_iota(jnp.int32, (64, 256), 1)
    later = (col < 64) & (row // NODE == col // NODE) & (col > row)

    def load(chunk):
        for s in range(8):
            node = table[base + 8 + chunk * 8 + s]
            plane = lax.rem(z - node // 8 + N_Z, N_Z)
            start = pl.multiple_of(plane * 64 + (node % 2) * NODE, NODE)
            kv_scr[s * NODE : (s + 1) * NODE] = kv[(node % 8) // 2, pl.ds(start, NODE), :]
        cols = pl.ds(pl.multiple_of(chunk * 256, 256), 256)
        mask = jnp.where(row < NODE, seen[0, 0:1, cols], seen[0, 1:2, cols]) < 0.5
        scores = (
            lax.dot_general(
                queries, kv_scr[:, :128], (((1,), (1,)), ((), ())), preferred_element_type=F32
            )
            * inv_scale
        )
        return scores.reshape(4, 64, 256), mask

    scores, mask = load(0)
    scores = jnp.where((mask | later)[None], MASKED, scores).reshape(256, 256)
    top = jnp.max(scores, axis=-1, keepdims=True)
    probs = jnp.exp(scores - top)
    total = jnp.sum(probs, axis=-1, keepdims=True)
    mixed = jnp.dot(probs.astype(BF16), kv_scr[:, 128:], preferred_element_type=F32)

    def step(chunk, carry):
        top, total, mixed = carry
        scores, mask = load(chunk)
        scores = jnp.where(mask[None], MASKED, scores).reshape(256, 256)
        new_top = jnp.maximum(top, jnp.max(scores, axis=-1, keepdims=True))
        old = jnp.exp(top - new_top)
        probs = jnp.exp(scores - new_top)
        total = old * total + jnp.sum(probs, axis=-1, keepdims=True)
        mixed = old * mixed + jnp.dot(
            probs.astype(BF16), kv_scr[:, 128:], preferred_element_type=F32
        )
        return new_top, total, mixed

    chunks = (table[base] + 7) // 8
    top, total, mixed = lax.fori_loop(1, chunks, step, (top, total, mixed))
    attended = (mixed / total).astype(BF16)
    for h in range(4):
        att[pl.ds(pl.multiple_of(k * 64, 64), 64), h * 128 : (h + 1) * 128] = attended[
            h * 64 : (h + 1) * 64
        ]

    @pl.when(k == N_Z - 1)
    def _():
        out[...] = jnp.dot(att[...], w_scr[...], preferred_element_type=F32).astype(BF16)


def attend(table, q, kv, seen, wo_own, wo_rest):
    whole = lambda shape: pl.BlockSpec(shape, lambda i, s: (0,) * len(shape))
    return pl.pallas_call(
        attend_kernel,
        out_shape=jax.ShapeDtypeStruct((512, 2048), BF16),
        grid_spec=pltpu.PrefetchScalarGridSpec(
            num_scalar_prefetch=1,
            grid=(N_Z,),
            in_specs=[
                pl.BlockSpec((4, 64, 128), lambda i, s: (0, i, 0)),
                whole((N_Y, 512, 256)),
                pl.BlockSpec((1, 2, 2048), lambda i, s: (i, 0, 0)),
                whole((128, 2048)),
                whole((384, 2048)),
            ],
            out_specs=whole((512, 2048)),
            scratch_shapes=[
                pltpu.VMEM((512, 512), BF16),
                pltpu.VMEM((512, 2048), BF16),
                pltpu.VMEM((256, 256), BF16),
            ],
        ),
        compiler_params=pltpu.CompilerParams(vmem_limit_bytes=VMEM_LIMIT),
        name="attend",
    )(table, q, kv, seen, wo_own, wo_rest)


def route_kernel(place, meta, spread_out, gate_out):
    slots = spread_out.shape[0]
    rows = meta.shape[0]
    per = slots // 16
    z = place[0]
    info = meta[...].astype(F32)
    member = lax.broadcasted_iota(jnp.int32, (1, 128), 1)
    expert = (member // N_Y) * (N_Z * N_Y) + z * N_Y + member % N_Y
    expert = jnp.where(member < 16, expert, -1).astype(F32)
    hot = jnp.zeros((rows, 128), F32)
    high = jnp.zeros((rows, 128), F32)
    for i in range(8):
        same = info[:, i : i + 1] == expert
        hot = hot + jnp.where(same, 1.0, 0.0)
        high = high + jnp.where(same, info[:, 8 + i : 9 + i], 0.0)
    upto = lax.broadcasted_iota(jnp.int32, (rows, rows), 0) >= lax.broadcasted_iota(
        jnp.int32, (rows, rows), 1
    )
    count = jnp.dot(
        jnp.where(upto, 1.0, 0.0).astype(BF16), hot.astype(BF16), preferred_element_type=F32
    )
    rank = (count * hot).astype(BF16)
    slot_of = lax.broadcasted_iota(jnp.int32, (128, slots), 1) // per
    grow = jnp.where(
        slot_of == lax.broadcasted_iota(jnp.int32, (128, slots), 0), 1.0, 0.0
    ).astype(BF16)
    wide = jnp.dot(rank, grow, preferred_element_type=F32)
    nth = (lax.broadcasted_iota(jnp.int32, (1, slots), 1) % per + 1).astype(F32)
    at = wide == nth
    gate_out[...] = jnp.where(
        at, jnp.dot(high.astype(BF16), grow, preferred_element_type=F32), 0.0
    ).astype(BF16)
    spread_out[...] = jnp.where(at, 1.0, 0.0).T.astype(BF16)


def route(place, meta, slots):
    rows = meta.shape[0]
    whole = lambda shape: pl.BlockSpec(shape, lambda i, s: (0,) * len(shape))
    return pl.pallas_call(
        route_kernel,
        out_shape=(
            jax.ShapeDtypeStruct((slots, rows), BF16),
            jax.ShapeDtypeStruct((rows, slots), BF16),
        ),
        grid_spec=pltpu.PrefetchScalarGridSpec(
            num_scalar_prefetch=1,
            grid=(1,),
            in_specs=[whole(meta.shape)],
            out_specs=(whole((slots, rows)), whole((rows, slots))),
        ),
        compiler_params=pltpu.CompilerParams(vmem_limit_bytes=VMEM_LIMIT),
        name="route",
    )(place, meta)


def ffn_kernel(x, gate_up, down, out):
    rows = x[...]
    gate = jnp.dot(rows, gate_up[0], preferred_element_type=F32)
    up = jnp.dot(rows, gate_up[1], preferred_element_type=F32)
    hidden = (gate / (1.0 + jnp.exp(-gate)) * up).astype(BF16)
    out[...] = jnp.dot(hidden, down[...], preferred_element_type=F32).astype(BF16)


def ffn(x, gate_up, down):
    rows = 256
    whole = lambda shape: pl.BlockSpec(
        shape, lambda i: (0,) * len(shape), pipeline_mode=pl.Buffered(1)
    )
    return pl.pallas_call(
        ffn_kernel,
        out_shape=jax.ShapeDtypeStruct(x.shape, BF16),
        grid=(x.shape[0] // rows,),
        in_specs=[
            pl.BlockSpec((rows, 2048), lambda i: (i, 0)),
            whole(gate_up.shape),
            whole(down.shape),
        ],
        out_specs=pl.BlockSpec((rows, 2048), lambda i: (i, 0)),
        compiler_params=pltpu.CompilerParams(vmem_limit_bytes=VMEM_LIMIT),
        name="ffn",
    )(x, gate_up, down)


def combine_kernel(g, r, out):
    out[...] = jnp.dot(g[...], r[...], preferred_element_type=F32).astype(BF16)


def combine(g, r):
    cols = 512
    return pl.pallas_call(
        combine_kernel,
        out_shape=jax.ShapeDtypeStruct((g.shape[0], r.shape[1]), BF16),
        grid=(r.shape[1] // cols,),
        in_specs=[
            pl.BlockSpec(g.shape, lambda i: (0, 0)),
            pl.BlockSpec((r.shape[0], cols), lambda i: (0, i)),
        ],
        out_specs=pl.BlockSpec((g.shape[0], cols), lambda i: (0, i)),
        compiler_params=pltpu.CompilerParams(vmem_limit_bytes=VMEM_LIMIT),
        name="combine",
    )(g, r)


def ancestry(parent_row):
    nodes = parent_row.shape[0]
    ids = jnp.arange(nodes, dtype=jnp.int32)
    reach = ((parent_row[:, None] == ids[None, :]) | (ids[:, None] == ids[None, :])).astype(BF16)
    for _ in range((nodes - 1).bit_length()):
        reach = (jnp.dot(reach, reach, preferred_element_type=F32) > 0.5).astype(BF16)
    return reach


def body(
    tokens,
    parents,
    route_ids,
    route_gates,
    input_gain,
    q_gain,
    k_gain,
    post_gain,
    w_query,
    w_keyval,
    w_out,
    w_gate_up,
    w_down,
):
    z = lax.axis_index("z")
    y = lax.axis_index("y")
    role = lax.axis_index("role")
    place = jnp.stack([z, y]).astype(jnp.int32)
    half = 1024
    swap = [(0, 1), (1, 0)]

    meta = jnp.concatenate(
        [route_ids[0].astype(BF16), route_gates[0].astype(BF16), jnp.zeros((64, 112), BF16)], axis=1
    )
    own = tokens[0]
    gate_up_b = lax.ppermute(w_gate_up[0], "role", swap)
    down_b = lax.ppermute(w_down[0], "role", swap)
    xa, (gate_up_b, down_b) = ring_gather(own[:, :half], (gate_up_b, down_b))
    xb = ring_gather(jnp.concatenate([own[:, half:], meta], axis=1))
    meta_col = xb[:, half:]

    wq_own = w_query.T
    mine = jnp.where(role == 0, wq_own, w_out)
    mine = jnp.concatenate([shift(mine, "y", N_Y, k) for k in (1, 3, 2)], axis=0)
    theirs = lax.ppermute(mine, "role", swap)
    wq_rest = jnp.where(role == 0, mine, theirs)
    wo_rest = jnp.where(role == 0, theirs, mine)

    reach = ancestry(parents[0])
    depth = jnp.sum(reach.astype(F32), axis=1) - 1.0
    node_ids = jnp.arange(64, dtype=jnp.int32)
    t512 = jnp.arange(512, dtype=jnp.int32)
    node_of = ((z - t512 // 64) % N_Z) * 8 + y * 2 + (t512 % 64) // NODE
    depth_of = jnp.sum(
        jnp.where(node_of[:, None] == node_ids[None, :], depth[None, :], 0.0), axis=1
    )
    positions = depth_of * NODE + (t512 % NODE).astype(F32)
    frequency = jnp.power(ROPE_BASE, -2.0 * jnp.arange(64, dtype=F32) / 128)
    angles = positions[:, None] * frequency[None, :]
    cosine = jnp.cos(angles)
    sine = jnp.sin(angles)
    cosd = jnp.concatenate([cosine, cosine], axis=1)
    sind = jnp.concatenate([-sine, sine], axis=1)

    first = ((z - jnp.arange(8, dtype=jnp.int32)) % N_Z) * 8 + y * 2
    is_a = (first[:, None] == node_ids[None, :]).astype(BF16)
    is_b = (first[:, None] + 1 == node_ids[None, :]).astype(BF16)
    see_a = jnp.dot(is_a, reach, preferred_element_type=F32)
    see_b = jnp.dot(is_b, reach, preferred_element_type=F32)
    own_two = (is_a + is_b).astype(F32)
    others = jnp.where(own_two > 0.5, 0.0, jnp.maximum(see_a, see_b))
    before = (node_ids[:, None] < node_ids[None, :]).astype(BF16)
    rank = jnp.dot(others.astype(BF16), before, preferred_element_type=F32) + 2.0
    at = jnp.where(others > 0.5, rank, jnp.where(own_two > 0.5, is_b.astype(F32), -1.0))
    listed = (at[:, :, None] == node_ids.astype(F32)[None, None, :]).astype(F32)
    nodes = jnp.sum(listed * node_ids.astype(F32)[None, :, None], axis=1).astype(jnp.int32)
    count = jnp.sum(others, axis=1).astype(jnp.int32) + 2
    table = jnp.concatenate(
        [jnp.broadcast_to(count[:, None], (8, 8)), nodes], axis=1
    ).reshape(-1)
    table = jnp.concatenate([jnp.broadcast_to(z, (8,)).astype(jnp.int32), table])
    vis = jnp.stack(
        [jnp.sum(listed * see_a[:, :, None], axis=1), jnp.sum(listed * see_b[:, :, None], axis=1)],
        axis=1,
    ).reshape(16, 64)
    grow = (node_ids[:, None] == jnp.arange(2048, dtype=jnp.int32)[None, :] // NODE).astype(BF16)
    seen = jnp.dot(vis.astype(BF16), grow, preferred_element_type=F32).reshape(8, 2, 2048)

    kv, normed = project_kv(
        (z // 2).reshape(1).astype(jnp.int32),
        xa,
        xb,
        input_gain.reshape(1, -1),
        w_keyval,
        cosd,
        sind,
        k_gain.reshape(1, -1),
    )
    kv_all = lax.all_to_all(kv, "y", 0, 0, tiled=True)
    q = project_q(normed, wq_own, wq_rest, cosd, sind, q_gain.reshape(1, -1))
    partial = attend(table, q, kv_all, seen, w_out, wo_rest).reshape(8, 64, 2048)
    attn = jnp.concatenate(
        [ring_scatter(partial[:, :, :half]), ring_scatter(partial[:, :, half:])], axis=1
    )
    middle = (own.astype(F32) + attn).astype(BF16)
    middle_f = middle.astype(F32)
    post_normed = rms_scale(middle_f, post_gain).astype(BF16)

    slots = 16 * CAP * N_Z
    spread, gate = route(place, meta_col, slots)
    pa = ring_gather(post_normed[:, :half])
    pb = ring_gather(post_normed[:, half:])
    outgoing = jnp.dot(
        spread, jnp.concatenate([pa, pb], axis=1), preferred_element_type=F32
    ).astype(BF16)
    received = lax.all_to_all(
        outgoing.reshape(16, CAP * N_Z, 2048), ("grp", "y"), 0, 0, tiled=True
    )
    gate_up = jnp.concatenate([w_gate_up[0], gate_up_b], axis=2)
    down = jnp.concatenate([w_down[0], down_b], axis=0)
    result = ffn(received.reshape(slots, 2048), gate_up, down)
    returned = lax.all_to_all(
        result.reshape(16, CAP * N_Z, 2048), ("grp", "y"), 0, 0, tiled=True
    )
    moe_part = combine(gate, returned.reshape(slots, 2048)).reshape(8, 64, 2048)
    moe = jnp.concatenate(
        [ring_scatter(moe_part[:, :, :half]), ring_scatter(moe_part[:, :, half:])], axis=1
    )
    return (middle_f + moe).astype(BF16)[None]


def solution(mesh):
    split = Mesh(mesh.devices.reshape(2, 4, 8, 4), ("role", "grp", "z", "y"))
    seq = ("z", "y")
    in_specs = (
        P(("role", "grp"), seq, None),
        P(("role", "grp"), None),
        P(("role", "grp"), seq, None),
        P(("role", "grp"), seq, None),
        P(),
        P(),
        P(),
        P(),
        P(None, seq),
        P(),
        P(seq, None),
        P(("grp", "z", "y"), None, None, "role"),
        P(("grp", "z", "y"), "role", None),
    )
    out_specs = P(("role", "grp"), seq, None)
    return jax.shard_map(body, mesh=split, in_specs=in_specs, out_specs=out_specs, check_vma=False)
```

```python
import functools
import math

import jax
import jax.numpy as jnp
from jax import lax
from jax.experimental import pallas as pl
from jax.experimental.pallas import tpu as pltpu
from jax.sharding import Mesh, PartitionSpec as P

NODE = 32
CAP = 6
EPSILON = 1e-06
ROPE_BASE = 1000000.0
MASKED = -1e30
BF16 = jnp.bfloat16
F32 = jnp.float32
N_Z = 8
N_Y = 4
N_X = 4
VMEM_LIMIT = 60 * 1024 * 1024


def shift(x, axis, size, by):
    return lax.ppermute(x, axis, [(i, (i + by) % size) for i in range(size)])


def plane_gather(x):
    copies = jnp.broadcast_to(x[None], (N_Z,) + x.shape)
    got = lax.all_to_all(copies, "z", 0, 0, tiled=True)
    return got.reshape(N_Z * x.shape[0], x.shape[1])


def plane_sum(parts):
    blocks = parts.reshape(N_Z, parts.shape[0] // N_Z, parts.shape[1])
    got = lax.all_to_all(blocks, "z", 0, 0, tiled=True)
    return jnp.sum(got.astype(F32), axis=0)


def rms_scale(values, gain):
    mean_sq = jnp.mean(values * values, axis=-1, keepdims=True)
    return values * lax.rsqrt(mean_sq + EPSILON) * gain


def kv_kernel(kv_ref, x, gain, wkv, cosd, sind, kg, kv_out, n_out):
    normed = rms_scale(x[:, :2048].astype(F32), gain[...]).astype(BF16)
    n_out[...] = normed
    proj = jnp.dot(normed, wkv[0], preferred_element_type=F32)
    proj = proj.astype(BF16)
    u = rms_scale(proj[:, :128].astype(F32), kg[...])
    keys = (u * cosd[...] + pltpu.roll(u, 64, 1) * sind[...]).astype(BF16)
    for copy in range(N_Y):
        kv_out[copy, :, :128] = keys
        kv_out[copy, :, 128:] = proj[:, 128:]


def project_kv(kv_index, x, gain, w_keyval, cosd, sind, k_gain):
    rows = 256
    total = x.shape[0]
    whole = lambda shape: pl.BlockSpec(shape, lambda i, s: (0,) * len(shape))
    return pl.pallas_call(
        kv_kernel,
        out_shape=(
            jax.ShapeDtypeStruct((N_Y, total, 256), BF16),
            jax.ShapeDtypeStruct((total, 2048), BF16),
        ),
        grid_spec=pltpu.PrefetchScalarGridSpec(
            num_scalar_prefetch=1,
            grid=(total // rows,),
            in_specs=[
                pl.BlockSpec((rows, x.shape[1]), lambda i, s: (i, 0)),
                whole((1, 2048)),
                pl.BlockSpec((1, 2048, 256), lambda i, s: (s[0], 0, 0)),
                pl.BlockSpec((rows, 128), lambda i, s: (i, 0)),
                pl.BlockSpec((rows, 128), lambda i, s: (i, 0)),
                whole((1, 128)),
            ],
            out_specs=(
                pl.BlockSpec((N_Y, rows, 256), lambda i, s: (0, i, 0)),
                pl.BlockSpec((rows, 2048), lambda i, s: (i, 0)),
            ),
        ),
        compiler_params=pltpu.CompilerParams(vmem_limit_bytes=VMEM_LIMIT),
        name="project_kv",
    )(kv_index, x, gain, w_keyval, cosd, sind, k_gain)


def q_kernel(n, wq_own, wq_rest, cosd, sind, qg, q_out, w_scr):
    @pl.when(pl.program_id(0) == 0)
    def _():
        w_scr[:128] = wq_own[...]
        w_scr[128:] = wq_rest[...]

    proj = lax.dot_general(
        n[...], w_scr[...], (((1,), (1,)), ((), ())), preferred_element_type=F32
    ).astype(BF16)
    cos = cosd[...]
    sin = sind[...]
    for h in range(4):
        u = rms_scale(proj[:, h * 128 : (h + 1) * 128].astype(F32), qg[...])
        q_out[h] = (u * cos + pltpu.roll(u, 64, 1) * sin).astype(BF16)


def project_q(n, wq_own, wq_rest, cosd, sind, q_gain):
    rows = 256
    total = n.shape[0]
    whole = lambda shape: pl.BlockSpec(shape, lambda i: (0,) * len(shape))
    return pl.pallas_call(
        q_kernel,
        out_shape=jax.ShapeDtypeStruct((4, total, 128), BF16),
        grid=(total // rows,),
        in_specs=[
            pl.BlockSpec((rows, 2048), lambda i: (i, 0)),
            whole((128, 2048)),
            whole((384, 2048)),
            pl.BlockSpec((rows, 128), lambda i: (i, 0)),
            pl.BlockSpec((rows, 128), lambda i: (i, 0)),
            whole((1, 128)),
        ],
        out_specs=pl.BlockSpec((4, rows, 128), lambda i: (0, i, 0)),
        scratch_shapes=[pltpu.VMEM((512, 2048), BF16)],
        compiler_params=pltpu.CompilerParams(vmem_limit_bytes=VMEM_LIMIT),
        name="project_q",
    )(n, wq_own, wq_rest, cosd, sind, q_gain)


def attend_kernel(table, q, kv, seen, wo_own, wo_rest, out, att, w_scr, kv_scr):
    k = pl.program_id(0)
    base = k * 72

    @pl.when(k == 0)
    def _():
        w_scr[:128] = wo_own[...]
        w_scr[128:] = wo_rest[...]

    queries = q[...].reshape(256, 128)
    inv_scale = 1.0 / math.sqrt(128)
    row = lax.broadcasted_iota(jnp.int32, (64, 256), 0)
    col = lax.broadcasted_iota(jnp.int32, (64, 256), 1)
    later = (col < 64) & (row // NODE == col // NODE) & (col > row)

    def load(chunk):
        for s in range(8):
            node = table[base + 8 + chunk * 8 + s]
            start = pl.multiple_of((node // 8) * 64 + (node % 2) * NODE, NODE)
            kv_scr[s * NODE : (s + 1) * NODE] = kv[(node % 8) // 2, pl.ds(start, NODE), :]
        cols = pl.ds(pl.multiple_of(chunk * 256, 256), 256)
        mask = jnp.where(row < NODE, seen[0, 0:1, cols], seen[0, 1:2, cols]) < 0.5
        scores = (
            lax.dot_general(
                queries, kv_scr[:, :128], (((1,), (1,)), ((), ())), preferred_element_type=F32
            )
            * inv_scale
        )
        return scores.reshape(4, 64, 256), mask

    scores, mask = load(0)
    scores = jnp.where((mask | later)[None], MASKED, scores).reshape(256, 256)
    top = jnp.max(scores, axis=-1, keepdims=True)
    probs = jnp.exp(scores - top)
    total = jnp.sum(probs, axis=-1, keepdims=True)
    mixed = jnp.dot(probs.astype(BF16), kv_scr[:, 128:], preferred_element_type=F32)

    def step(chunk, carry):
        top, total, mixed = carry
        scores, mask = load(chunk)
        scores = jnp.where(mask[None], MASKED, scores).reshape(256, 256)
        new_top = jnp.maximum(top, jnp.max(scores, axis=-1, keepdims=True))
        old = jnp.exp(top - new_top)
        probs = jnp.exp(scores - new_top)
        total = old * total + jnp.sum(probs, axis=-1, keepdims=True)
        mixed = old * mixed + jnp.dot(
            probs.astype(BF16), kv_scr[:, 128:], preferred_element_type=F32
        )
        return new_top, total, mixed

    chunks = (table[base] + 7) // 8
    top, total, mixed = lax.fori_loop(1, chunks, step, (top, total, mixed))
    attended = (mixed / total).astype(BF16)
    for h in range(4):
        att[pl.ds(pl.multiple_of(k * 64, 64), 64), h * 128 : (h + 1) * 128] = attended[
            h * 64 : (h + 1) * 64
        ]

    @pl.when(k == N_Z - 1)
    def _():
        out[...] = jnp.dot(att[...], w_scr[...], preferred_element_type=F32).astype(BF16)


def attend(table, q, kv, seen, wo_own, wo_rest):
    whole = lambda shape: pl.BlockSpec(shape, lambda i, s: (0,) * len(shape))
    return pl.pallas_call(
        attend_kernel,
        out_shape=jax.ShapeDtypeStruct((512, 2048), BF16),
        grid_spec=pltpu.PrefetchScalarGridSpec(
            num_scalar_prefetch=1,
            grid=(N_Z,),
            in_specs=[
                pl.BlockSpec((4, 64, 128), lambda i, s: (0, i, 0)),
                whole((N_Y, 512, 256)),
                pl.BlockSpec((1, 2, 2048), lambda i, s: (i, 0, 0)),
                whole((128, 2048)),
                whole((384, 2048)),
            ],
            out_specs=whole((512, 2048)),
            scratch_shapes=[
                pltpu.VMEM((512, 512), BF16),
                pltpu.VMEM((512, 2048), BF16),
                pltpu.VMEM((256, 256), BF16),
            ],
        ),
        compiler_params=pltpu.CompilerParams(vmem_limit_bytes=VMEM_LIMIT),
        name="attend",
    )(table, q, kv, seen, wo_own, wo_rest)


def route_kernel(place, meta, spread_out, gate_out):
    slots = spread_out.shape[0]
    rows = meta.shape[0]
    per = slots // 16
    z = place[0]
    info = meta[...].astype(F32)
    member = lax.broadcasted_iota(jnp.int32, (1, 128), 1)
    expert = (member // N_Y) * (N_Z * N_Y) + z * N_Y + member % N_Y
    expert = jnp.where(member < 16, expert, -1).astype(F32)
    hot = jnp.zeros((rows, 128), F32)
    high = jnp.zeros((rows, 128), F32)
    for i in range(8):
        same = info[:, i : i + 1] == expert
        hot = hot + jnp.where(same, 1.0, 0.0)
        high = high + jnp.where(same, info[:, 8 + i : 9 + i], 0.0)
    upto = lax.broadcasted_iota(jnp.int32, (rows, rows), 0) >= lax.broadcasted_iota(
        jnp.int32, (rows, rows), 1
    )
    count = jnp.dot(
        jnp.where(upto, 1.0, 0.0).astype(BF16), hot.astype(BF16), preferred_element_type=F32
    )
    rank = (count * hot).astype(BF16)
    slot_of = lax.broadcasted_iota(jnp.int32, (128, slots), 1) // per
    grow = jnp.where(
        slot_of == lax.broadcasted_iota(jnp.int32, (128, slots), 0), 1.0, 0.0
    ).astype(BF16)
    wide = jnp.dot(rank, grow, preferred_element_type=F32)
    nth = (lax.broadcasted_iota(jnp.int32, (1, slots), 1) % per + 1).astype(F32)
    at = wide == nth
    gate_out[...] = jnp.where(
        at, jnp.dot(high.astype(BF16), grow, preferred_element_type=F32), 0.0
    ).astype(BF16)
    spread_out[...] = jnp.where(at, 1.0, 0.0).T.astype(BF16)


def route(place, meta, slots):
    rows = meta.shape[0]
    whole = lambda shape: pl.BlockSpec(shape, lambda i, s: (0,) * len(shape))
    return pl.pallas_call(
        route_kernel,
        out_shape=(
            jax.ShapeDtypeStruct((slots, rows), BF16),
            jax.ShapeDtypeStruct((rows, slots), BF16),
        ),
        grid_spec=pltpu.PrefetchScalarGridSpec(
            num_scalar_prefetch=1,
            grid=(1,),
            in_specs=[pl.BlockSpec((rows, 128), lambda i, s: (0, meta.shape[1] // 128 - 1))],
            out_specs=(whole((slots, rows)), whole((rows, slots))),
        ),
        compiler_params=pltpu.CompilerParams(vmem_limit_bytes=VMEM_LIMIT),
        name="route",
    )(place, meta)


def hidden_kernel(xa, xb, gate_up, down, hidden_out, out):
    half = xa.shape[1]

    def product(w):
        return jnp.dot(xa[...], w[:half], preferred_element_type=F32) + jnp.dot(
            xb[...], w[half:], preferred_element_type=F32
        )

    gate = product(gate_up.at[0])
    up = product(gate_up.at[1])
    hidden = (gate / (1.0 + jnp.exp(-gate)) * up).astype(BF16)
    hidden_out[...] = hidden
    out[...] = jnp.dot(hidden, down[...], preferred_element_type=F32).astype(BF16)


def ffn_first(xa, xb, gate_up, down):
    rows = 256
    half = xa.shape[1]
    ff = down.shape[0]
    total = xa.shape[0]
    once = pl.Buffered(1)
    return pl.pallas_call(
        hidden_kernel,
        out_shape=(
            jax.ShapeDtypeStruct((total, ff), BF16),
            jax.ShapeDtypeStruct((total, half), BF16),
        ),
        grid=(total // rows,),
        in_specs=[
            pl.BlockSpec((rows, half), lambda i: (i, 0)),
            pl.BlockSpec((rows, half), lambda i: (i, 0)),
            pl.BlockSpec(gate_up.shape, lambda i: (0, 0, 0), pipeline_mode=once),
            pl.BlockSpec((ff, half), lambda i: (0, 0), pipeline_mode=once),
        ],
        out_specs=(
            pl.BlockSpec((rows, ff), lambda i: (i, 0)),
            pl.BlockSpec((rows, half), lambda i: (i, 0)),
        ),
        compiler_params=pltpu.CompilerParams(vmem_limit_bytes=VMEM_LIMIT),
        name="ffn_first",
    )(xa, xb, gate_up, down)


def product_kernel(a, b, out):
    out[...] = jnp.dot(a[...], b[...], preferred_element_type=F32).astype(BF16)


def product(a, b, rows, half, at, name):
    return pl.pallas_call(
        product_kernel,
        out_shape=jax.ShapeDtypeStruct((a.shape[0], half), BF16),
        grid=(a.shape[0] // rows,),
        in_specs=[
            pl.BlockSpec((rows, a.shape[1]), lambda i: (i, 0)),
            pl.BlockSpec((b.shape[0], half), lambda i: (0, at)),
        ],
        out_specs=pl.BlockSpec((rows, half), lambda i: (i, 0)),
        compiler_params=pltpu.CompilerParams(vmem_limit_bytes=VMEM_LIMIT),
        name=name,
    )(a, b)


def ancestry(parent_row):
    nodes = parent_row.shape[0]
    ids = jnp.arange(nodes, dtype=jnp.int32)
    reach = ((parent_row[:, None] == ids[None, :]) | (ids[:, None] == ids[None, :])).astype(BF16)
    for _ in range((nodes - 1).bit_length()):
        reach = (jnp.dot(reach, reach, preferred_element_type=F32) > 0.5).astype(BF16)
    return reach


def body(
    tokens,
    parents,
    route_ids,
    route_gates,
    input_gain,
    q_gain,
    k_gain,
    post_gain,
    w_query,
    w_keyval,
    w_out,
    w_gate_up,
    w_down,
):
    z = lax.axis_index("z")
    y = lax.axis_index("y")
    role = lax.axis_index("role")
    place = jnp.stack([z, y]).astype(jnp.int32)
    half = 1024
    swap = [(0, 1), (1, 0)]

    meta = jnp.concatenate(
        [route_ids[0].astype(BF16), route_gates[0].astype(BF16), jnp.zeros((64, 112), BF16)], axis=1
    )
    own = tokens[0]
    gate_up_b = lax.ppermute(w_gate_up[0], "role", swap)
    down_b = lax.ppermute(w_down[0], "role", swap)
    x_all = plane_gather(jnp.concatenate([own, meta], axis=1))

    wq_own = w_query.T
    mine = jnp.where(role == 0, wq_own, w_out)
    mine = jnp.concatenate([shift(mine, "y", N_Y, k) for k in (1, 3, 2)], axis=0)
    theirs = lax.ppermute(mine, "role", swap)
    wq_rest = jnp.where(role == 0, mine, theirs)
    wo_rest = jnp.where(role == 0, theirs, mine)

    reach = ancestry(parents[0])
    depth = jnp.sum(reach.astype(F32), axis=1) - 1.0
    node_ids = jnp.arange(64, dtype=jnp.int32)
    t512 = jnp.arange(512, dtype=jnp.int32)
    node_of = (t512 // 64) * 8 + y * 2 + (t512 % 64) // NODE
    depth_of = jnp.sum(
        jnp.where(node_of[:, None] == node_ids[None, :], depth[None, :], 0.0), axis=1
    )
    positions = depth_of * NODE + (t512 % NODE).astype(F32)
    frequency = jnp.power(ROPE_BASE, -2.0 * jnp.arange(64, dtype=F32) / 128)
    angles = positions[:, None] * frequency[None, :]
    cosine = jnp.cos(angles)
    sine = jnp.sin(angles)
    cosd = jnp.concatenate([cosine, cosine], axis=1)
    sind = jnp.concatenate([-sine, sine], axis=1)

    first = jnp.arange(8, dtype=jnp.int32) * 8 + y * 2
    is_a = (first[:, None] == node_ids[None, :]).astype(BF16)
    is_b = (first[:, None] + 1 == node_ids[None, :]).astype(BF16)
    see_a = jnp.dot(is_a, reach, preferred_element_type=F32)
    see_b = jnp.dot(is_b, reach, preferred_element_type=F32)
    own_two = (is_a + is_b).astype(F32)
    others = jnp.where(own_two > 0.5, 0.0, jnp.maximum(see_a, see_b))
    before = (node_ids[:, None] < node_ids[None, :]).astype(BF16)
    rank = jnp.dot(others.astype(BF16), before, preferred_element_type=F32) + 2.0
    at = jnp.where(others > 0.5, rank, jnp.where(own_two > 0.5, is_b.astype(F32), -1.0))
    listed = (at[:, :, None] == node_ids.astype(F32)[None, None, :]).astype(F32)
    nodes = jnp.sum(listed * node_ids.astype(F32)[None, :, None], axis=1).astype(jnp.int32)
    count = jnp.sum(others, axis=1).astype(jnp.int32) + 2
    table = jnp.concatenate(
        [jnp.broadcast_to(count[:, None], (8, 8)), nodes], axis=1
    ).reshape(-1)
    vis = jnp.stack(
        [jnp.sum(listed * see_a[:, :, None], axis=1), jnp.sum(listed * see_b[:, :, None], axis=1)],
        axis=1,
    ).reshape(16, 64)
    grow = (node_ids[:, None] == jnp.arange(2048, dtype=jnp.int32)[None, :] // NODE).astype(BF16)
    seen = jnp.dot(vis.astype(BF16), grow, preferred_element_type=F32).reshape(8, 2, 2048)

    kv, normed = project_kv(
        (z // 2).reshape(1).astype(jnp.int32),
        x_all,
        input_gain.reshape(1, -1),
        w_keyval,
        cosd,
        sind,
        k_gain.reshape(1, -1),
    )
    kv_all = lax.all_to_all(kv, "y", 0, 0, tiled=True)
    q = project_q(normed, wq_own, wq_rest, cosd, sind, q_gain.reshape(1, -1))
    partial = attend(table, q, kv_all, seen, w_out, wo_rest)
    middle = (own.astype(F32) + plane_sum(partial)).astype(BF16)
    middle_f = middle.astype(F32)
    post_normed = rms_scale(middle_f, post_gain).astype(BF16)

    cap = CAP * N_Z
    slots = 16 * cap
    spread, gate = route(place, x_all, slots)
    received = []
    for part in (post_normed[:, :half], post_normed[:, half:]):
        rows = product(spread, plane_gather(part), 384, half, 0, "spread")
        got = lax.all_to_all(rows.reshape(16, cap, half), ("grp", "y"), 0, 0, tiled=True)
        received.append(got.reshape(slots, half))
    gate_up = jnp.concatenate([w_gate_up[0], gate_up_b], axis=2)
    down = jnp.concatenate([w_down[0], down_b], axis=0)
    hidden, result_a = ffn_first(received[0], received[1], gate_up, down)
    result_b = product(hidden, down, 256, half, 1, "ffn_second")
    moe = []
    for part in (result_a, result_b):
        got = lax.all_to_all(part.reshape(16, cap, half), ("grp", "y"), 0, 0, tiled=True)
        moe.append(plane_sum(product(gate, got.reshape(slots, half), 256, half, 0, "combine")))
    return (middle_f + jnp.concatenate(moe, axis=1)).astype(BF16)[None]


def solution(mesh):
    split = Mesh(mesh.devices.reshape(2, 4, 8, 4), ("role", "grp", "z", "y"))
    seq = ("z", "y")
    in_specs = (
        P(("role", "grp"), seq, None),
        P(("role", "grp"), None),
        P(("role", "grp"), seq, None),
        P(("role", "grp"), seq, None),
        P(),
        P(),
        P(),
        P(),
        P(None, seq),
        P(),
        P(seq, None),
        P(("grp", "z", "y"), None, None, "role"),
        P(("grp", "z", "y"), "role", None),
    )
    out_specs = P(("role", "grp"), seq, None)
    return jax.shard_map(body, mesh=split, in_specs=in_specs, out_specs=out_specs, check_vma=False)
```

```python
import math

import jax
import jax.numpy as jnp
from jax import lax
from jax.experimental import pallas as pl
from jax.experimental.pallas import tpu as pltpu
from jax.sharding import Mesh, PartitionSpec as P


NODE = 32
CAP = 6
EPSILON = 1e-06
ROPE_BASE = 1000000.0
MASKED = -1e30
BF16 = jnp.bfloat16
F32 = jnp.float32
N_Z = 8
N_Y = 4
VMEM_LIMIT = 60 * 1024 * 1024


def shift(x, axis, size, by):
    return lax.ppermute(x, axis, [(i, (i + by) % size) for i in range(size)])


def ring_gather(x):
    fwd, bwd = [x], [x]
    for step in range(4):
        fwd.append(shift(fwd[-1], "z", N_Z, 1))
        if step < 3:
            bwd.append(shift(bwd[-1], "z", N_Z, N_Z - 1))
    return fwd + bwd[:0:-1]


def ring_scatter(slabs):
    def plus(a, b):
        return (a.astype(F32) + b.astype(F32)).astype(BF16)

    fwd, bwd = slabs[4], slabs[3]
    for step in range(4):
        fwd = shift(fwd, "z", N_Z, 1)
        if step < 3:
            fwd = plus(fwd, slabs[5 + step])
            bwd = shift(bwd, "z", N_Z, N_Z - 1)
        if step < 2:
            bwd = plus(bwd, slabs[2 - step])
    return fwd.astype(F32) + bwd.astype(F32) + slabs[0].astype(F32)


def rms_scale(values, gain):
    mean_sq = jnp.mean(values * values, axis=-1, keepdims=True)
    return values * lax.rsqrt(mean_sq + EPSILON) * gain


def kv_kernel(kv_ref, *refs):
    pieces_a, pieces_b = refs[:N_Z], refs[N_Z : 2 * N_Z]
    gain, wkv, cosd, sind, kg, kv_out, n_out, meta_out = refs[2 * N_Z :]
    width = pieces_a[0].shape[1]
    for k in range(N_Z):
        rows = slice(k * 64, (k + 1) * 64)
        fa = pieces_a[k][...].astype(F32)
        fb = pieces_b[k][:, :width].astype(F32)
        mean_sq = (
            jnp.sum(fa * fa, axis=-1, keepdims=True) + jnp.sum(fb * fb, axis=-1, keepdims=True)
        ) / (2 * width)
        scale = lax.rsqrt(mean_sq + EPSILON)
        n_out[rows, :width] = (fa * scale * gain[:, :width]).astype(BF16)
        n_out[rows, width:] = (fb * scale * gain[:, width:]).astype(BF16)
        meta_out[rows] = pieces_b[k][:, width:]
    proj = jnp.dot(n_out[...], wkv[0], preferred_element_type=F32).astype(BF16)
    u = rms_scale(proj[:, :128].astype(F32), kg[...])
    keys = (u * cosd[...] + pltpu.roll(u, 64, 1) * sind[...]).astype(BF16)
    for copy in range(N_Y):
        kv_out[copy, :, :128] = keys
        kv_out[copy, :, 128:] = proj[:, 128:]


def project_kv(kv_index, xa, xb, gain, w_keyval, cosd, sind, k_gain):
    total = 64 * N_Z
    whole = lambda shape: pl.BlockSpec(shape, lambda i, s: (0,) * len(shape))
    return pl.pallas_call(
        kv_kernel,
        out_shape=(
            jax.ShapeDtypeStruct((N_Y, total, 256), BF16),
            jax.ShapeDtypeStruct((total, 2048), BF16),
            jax.ShapeDtypeStruct((total, 128), BF16),
        ),
        grid_spec=pltpu.PrefetchScalarGridSpec(
            num_scalar_prefetch=1,
            grid=(1,),
            in_specs=[whole(p.shape) for p in xa + xb]
            + [
                whole((1, 2048)),
                pl.BlockSpec((1, 2048, 256), lambda i, s: (s[0], 0, 0)),
                whole((total, 128)),
                whole((total, 128)),
                whole((1, 128)),
            ],
            out_specs=(
                whole((N_Y, total, 256)),
                whole((total, 2048)),
                whole((total, 128)),
            ),
        ),
        compiler_params=pltpu.CompilerParams(vmem_limit_bytes=VMEM_LIMIT),
        name="project_kv",
    )(kv_index, *xa, *xb, gain, w_keyval, cosd, sind, k_gain)


def q_kernel(n, wq0, wq1, wq2, wq3, cosd, sind, qg, q_out, w_scr):
    @pl.when(pl.program_id(0) == 0)
    def _():
        for h, w in enumerate((wq0, wq1, wq2, wq3)):
            w_scr[:, h * 128 : (h + 1) * 128] = w[...]

    proj = jnp.dot(n[...], w_scr[...], preferred_element_type=F32).astype(BF16)
    cos = cosd[...]
    sin = sind[...]
    for h in range(4):
        u = rms_scale(proj[:, h * 128 : (h + 1) * 128].astype(F32), qg[...])
        q_out[h] = (u * cos + pltpu.roll(u, 64, 1) * sin).astype(BF16)


def project_q(n, wq, cosd, sind, q_gain):
    rows = 256
    total = n.shape[0]
    whole = lambda shape: pl.BlockSpec(shape, lambda i: (0,) * len(shape))
    return pl.pallas_call(
        q_kernel,
        out_shape=jax.ShapeDtypeStruct((4, total, 128), BF16),
        grid=(total // rows,),
        in_specs=[pl.BlockSpec((rows, 2048), lambda i: (i, 0))]
        + [whole((2048, 128))] * 4
        + [
            pl.BlockSpec((rows, 128), lambda i: (i, 0)),
            pl.BlockSpec((rows, 128), lambda i: (i, 0)),
            whole((1, 128)),
        ],
        out_specs=pl.BlockSpec((4, rows, 128), lambda i: (0, i, 0)),
        scratch_shapes=[pltpu.VMEM((2048, 512), BF16)],
        compiler_params=pltpu.CompilerParams(vmem_limit_bytes=VMEM_LIMIT),
        name="project_q",
    )(n, *wq, cosd, sind, q_gain)


def attend_kernel(table, q, kv, seen, wo0, wo1, wo2, wo3, out, att, w_scr, kv_scr):
    k = pl.program_id(0)
    z = table[0]
    base = 8 + k * 72

    @pl.when(k == 0)
    def _():
        for h, w in enumerate((wo0, wo1, wo2, wo3)):
            w_scr[h * 128 : (h + 1) * 128] = w[...]

    queries = q[...].reshape(256, 128)
    inv_scale = 1.0 / math.sqrt(128)
    row = lax.broadcasted_iota(jnp.int32, (64, 256), 0)
    col = lax.broadcasted_iota(jnp.int32, (64, 256), 1)
    later = (col < 64) & (row // NODE == col // NODE) & (col > row)

    def load(chunk):
        for s in range(8):
            node = table[base + 8 + chunk * 8 + s]
            plane = lax.rem(z - node // 8 + N_Z, N_Z)
            start = pl.multiple_of(plane * 64 + (node % 2) * NODE, NODE)
            kv_scr[s * NODE : (s + 1) * NODE] = kv[(node % 8) // 2, pl.ds(start, NODE), :]
        cols = pl.ds(pl.multiple_of(chunk * 256, 256), 256)
        mask = jnp.where(row < NODE, seen[0, 0:1, cols], seen[0, 1:2, cols]) < 0.5
        scores = (
            lax.dot_general(
                queries, kv_scr[:, :128], (((1,), (1,)), ((), ())), preferred_element_type=F32
            )
            * inv_scale
        )
        return scores.reshape(4, 64, 256), mask

    scores, mask = load(0)
    scores = jnp.where((mask | later)[None], MASKED, scores).reshape(256, 256)
    top = jnp.max(scores, axis=-1, keepdims=True)
    probs = jnp.exp(scores - top)
    total = jnp.sum(probs, axis=-1, keepdims=True)
    mixed = jnp.dot(probs.astype(BF16), kv_scr[:, 128:], preferred_element_type=F32)

    def step(chunk, carry):
        top, total, mixed = carry
        scores, mask = load(chunk)
        scores = jnp.where(mask[None], MASKED, scores).reshape(256, 256)
        new_top = jnp.maximum(top, jnp.max(scores, axis=-1, keepdims=True))
        old = jnp.exp(top - new_top)
        probs = jnp.exp(scores - new_top)
        total = old * total + jnp.sum(probs, axis=-1, keepdims=True)
        mixed = old * mixed + jnp.dot(
            probs.astype(BF16), kv_scr[:, 128:], preferred_element_type=F32
        )
        return new_top, total, mixed

    chunks = (table[base] + 7) // 8
    top, total, mixed = lax.fori_loop(1, chunks, step, (top, total, mixed))
    attended = (mixed / total).astype(BF16)
    for h in range(4):
        att[pl.ds(pl.multiple_of(k * 64, 64), 64), h * 128 : (h + 1) * 128] = attended[
            h * 64 : (h + 1) * 64
        ]

    @pl.when(k == N_Z - 1)
    def _():
        out[...] = jnp.dot(att[...], w_scr[...], preferred_element_type=F32).astype(BF16)


def attend(table, q, kv, seen, wo):
    whole = lambda shape: pl.BlockSpec(shape, lambda i, s: (0,) * len(shape))
    return pl.pallas_call(
        attend_kernel,
        out_shape=jax.ShapeDtypeStruct((512, 2048), BF16),
        grid_spec=pltpu.PrefetchScalarGridSpec(
            num_scalar_prefetch=1,
            grid=(N_Z,),
            in_specs=[
                pl.BlockSpec((4, 64, 128), lambda i, s: (0, i, 0)),
                whole((N_Y, 512, 256)),
                pl.BlockSpec((1, 2, 2048), lambda i, s: (i, 0, 0)),
                whole((128, 2048)),
                whole((128, 2048)),
                whole((128, 2048)),
                whole((128, 2048)),
            ],
            out_specs=whole((512, 2048)),
            scratch_shapes=[
                pltpu.VMEM((512, 512), BF16),
                pltpu.VMEM((512, 2048), BF16),
                pltpu.VMEM((256, 256), BF16),
            ],
        ),
        compiler_params=pltpu.CompilerParams(vmem_limit_bytes=VMEM_LIMIT),
        name="attend",
    )(table, q, kv, seen, *wo)


def route_kernel(place, meta, spread_out, gate_out):
    slots = spread_out.shape[0]
    rows = meta.shape[0]
    per = slots // 16
    z = place[0]
    info = meta[...].astype(F32)
    member = lax.broadcasted_iota(jnp.int32, (1, 128), 1)
    expert = (member // N_Y) * (N_Z * N_Y) + z * N_Y + member % N_Y
    expert = jnp.where(member < 16, expert, -1).astype(F32)
    hot = jnp.zeros((rows, 128), F32)
    high = jnp.zeros((rows, 128), F32)
    for i in range(8):
        same = info[:, i : i + 1] == expert
        hot = hot + jnp.where(same, 1.0, 0.0)
        high = high + jnp.where(same, info[:, 8 + i : 9 + i], 0.0)
    upto = lax.broadcasted_iota(jnp.int32, (rows, rows), 0) >= lax.broadcasted_iota(
        jnp.int32, (rows, rows), 1
    )
    count = jnp.dot(
        jnp.where(upto, 1.0, 0.0).astype(BF16), hot.astype(BF16), preferred_element_type=F32
    )
    rank = (count * hot).astype(BF16)
    slot_of = lax.broadcasted_iota(jnp.int32, (128, slots), 1) // per
    grow = jnp.where(
        slot_of == lax.broadcasted_iota(jnp.int32, (128, slots), 0), 1.0, 0.0
    ).astype(BF16)
    wide = jnp.dot(rank, grow, preferred_element_type=F32)
    nth = (lax.broadcasted_iota(jnp.int32, (1, slots), 1) % per + 1).astype(F32)
    at = wide == nth
    gate_out[...] = jnp.where(
        at, jnp.dot(high.astype(BF16), grow, preferred_element_type=F32), 0.0
    ).astype(BF16)
    spread_out[...] = jnp.where(at, 1.0, 0.0).T.astype(BF16)


def route(place, meta, slots):
    rows = meta.shape[0]
    whole = lambda shape: pl.BlockSpec(shape, lambda i, s: (0,) * len(shape))
    return pl.pallas_call(
        route_kernel,
        out_shape=(
            jax.ShapeDtypeStruct((slots, rows), BF16),
            jax.ShapeDtypeStruct((rows, slots), BF16),
        ),
        grid_spec=pltpu.PrefetchScalarGridSpec(
            num_scalar_prefetch=1,
            grid=(1,),
            in_specs=[whole(meta.shape)],
            out_specs=(whole((slots, rows)), whole((rows, slots))),
        ),
        compiler_params=pltpu.CompilerParams(vmem_limit_bytes=VMEM_LIMIT),
        name="route",
    )(place, meta)


def ffn_kernel(x, gu_a, gu_b, d_a, d_b, out, gate_up, down, sems):
    ff = d_a.shape[0]
    copies = []
    for part in range(2):
        for side, gu in enumerate((gu_a, gu_b)):
            copies.append((gu.at[part], gate_up.at[part, :, side * ff : (side + 1) * ff]))
    for side, d in enumerate((d_a, d_b)):
        copies.append((d, down.at[side * ff : (side + 1) * ff]))
    copies = [
        pltpu.make_async_copy(src, dst, sems.at[n]) for n, (src, dst) in enumerate(copies)
    ]
    first = pl.program_id(0) == 0

    def arrived(which):
        @pl.when(first)
        def _():
            for n in which:
                copies[n].wait()

    @pl.when(first)
    def _():
        for c in copies:
            c.start()

    rows = x[...]
    arrived((0, 1))
    gate = jnp.dot(rows, gate_up[0], preferred_element_type=F32)
    arrived((2, 3))
    up = jnp.dot(rows, gate_up[1], preferred_element_type=F32)
    hidden = (gate / (1.0 + jnp.exp(-gate)) * up).astype(BF16)
    arrived((4, 5))
    out[...] = jnp.dot(hidden, down[...], preferred_element_type=F32).astype(BF16)


def ffn(x, gu_a, gu_b, d_a, d_b):
    rows = 256
    ff, width = d_a.shape
    there = pl.BlockSpec(memory_space=pl.ANY)
    return pl.pallas_call(
        ffn_kernel,
        out_shape=jax.ShapeDtypeStruct(x.shape, BF16),
        grid=(x.shape[0] // rows,),
        in_specs=[pl.BlockSpec((rows, width), lambda i: (i, 0)), there, there, there, there],
        out_specs=pl.BlockSpec((rows, width), lambda i: (i, 0)),
        scratch_shapes=[
            pltpu.VMEM((2, width, 2 * ff), BF16),
            pltpu.VMEM((2 * ff, width), BF16),
            pltpu.SemaphoreType.DMA((6,)),
        ],
        compiler_params=pltpu.CompilerParams(vmem_limit_bytes=VMEM_LIMIT),
        name="ffn",
    )(x, gu_a, gu_b, d_a, d_b)


def spread_kernel(*refs):
    pieces_a, pieces_b = refs[:N_Z], refs[N_Z : 2 * N_Z]
    spread, out, rows = refs[2 * N_Z :]
    i = pl.program_id(0)

    def fill(pieces):
        for k in range(N_Z):
            rows[k * 64 : (k + 1) * 64] = pieces[k][...]

    pl.when(i == 0)(lambda: fill(pieces_a))
    pl.when(i == 1)(lambda: fill(pieces_b))
    out[...] = jnp.dot(spread[...], rows[...], preferred_element_type=F32).astype(BF16)


def spread_rows(spread, pa, pb):
    width = pa[0].shape[1]
    whole = lambda shape: pl.BlockSpec(shape, lambda i: (0,) * len(shape))
    return pl.pallas_call(
        spread_kernel,
        out_shape=jax.ShapeDtypeStruct((spread.shape[0], 2 * width), BF16),
        grid=(2,),
        in_specs=[whole(p.shape) for p in pa + pb] + [whole(spread.shape)],
        out_specs=pl.BlockSpec((spread.shape[0], width), lambda i: (0, i)),
        scratch_shapes=[pltpu.VMEM((spread.shape[1], width), BF16)],
        compiler_params=pltpu.CompilerParams(vmem_limit_bytes=VMEM_LIMIT),
        name="spread",
    )(*pa, *pb, spread)


def combine_kernel(g, r, out):
    out[...] = jnp.dot(g[...], r[...], preferred_element_type=F32).astype(BF16)


def combine(g, r):
    cols = 512
    return pl.pallas_call(
        combine_kernel,
        out_shape=jax.ShapeDtypeStruct((g.shape[0], r.shape[1]), BF16),
        grid=(r.shape[1] // cols,),
        in_specs=[
            pl.BlockSpec(g.shape, lambda i: (0, 0)),
            pl.BlockSpec((r.shape[0], cols), lambda i: (0, i)),
        ],
        out_specs=pl.BlockSpec((g.shape[0], cols), lambda i: (0, i)),
        compiler_params=pltpu.CompilerParams(vmem_limit_bytes=VMEM_LIMIT),
        name="combine",
    )(g, r)


def ancestry(parent_row):
    nodes = parent_row.shape[0]
    ids = jnp.arange(nodes, dtype=jnp.int32)
    reach = ((parent_row[:, None] == ids[None, :]) | (ids[:, None] == ids[None, :])).astype(BF16)
    for _ in range((nodes - 1).bit_length()):
        reach = (jnp.dot(reach, reach, preferred_element_type=F32) > 0.5).astype(BF16)
    return reach


def body(
    tokens,
    parents,
    route_ids,
    route_gates,
    input_gain,
    q_gain,
    k_gain,
    post_gain,
    w_query,
    w_keyval,
    w_out,
    w_gate_up,
    w_down,
):
    z = lax.axis_index("z")
    y = lax.axis_index("y")
    place = jnp.stack([z, y]).astype(jnp.int32)
    half = 1024
    swap = [(0, 1), (1, 0)]

    meta = jnp.concatenate(
        [route_ids[0].astype(BF16), route_gates[0].astype(BF16), jnp.zeros((64, 112), BF16)], axis=1
    )
    own = tokens[0]
    xa = ring_gather(own[:, :half])
    xb = ring_gather(jnp.concatenate([own[:, half:], meta], axis=1))
    wq = [w_query] + [shift(w_query, "y", N_Y, k) for k in (1, 3, 2)]
    wo = [w_out] + [shift(w_out, "y", N_Y, k) for k in (1, 3, 2)]

    reach = ancestry(parents[0])
    depth = jnp.sum(reach.astype(F32), axis=1) - 1.0
    node_ids = jnp.arange(64, dtype=jnp.int32)
    t512 = jnp.arange(512, dtype=jnp.int32)
    node_of = ((z - t512 // 64) % N_Z) * 8 + y * 2 + (t512 % 64) // NODE
    depth_of = jnp.sum(
        jnp.where(node_of[:, None] == node_ids[None, :], depth[None, :], 0.0), axis=1
    )
    positions = depth_of * NODE + (t512 % NODE).astype(F32)
    frequency = jnp.power(ROPE_BASE, -2.0 * jnp.arange(64, dtype=F32) / 128)
    angles = positions[:, None] * frequency[None, :]
    cosine = jnp.cos(angles)
    sine = jnp.sin(angles)
    cosd = jnp.concatenate([cosine, cosine], axis=1)
    sind = jnp.concatenate([-sine, sine], axis=1)

    first = ((z - jnp.arange(8, dtype=jnp.int32)) % N_Z) * 8 + y * 2
    is_a = (first[:, None] == node_ids[None, :]).astype(BF16)
    is_b = (first[:, None] + 1 == node_ids[None, :]).astype(BF16)
    see_a = jnp.dot(is_a, reach, preferred_element_type=F32)
    see_b = jnp.dot(is_b, reach, preferred_element_type=F32)
    own_two = (is_a + is_b).astype(F32)
    others = jnp.where(own_two > 0.5, 0.0, jnp.maximum(see_a, see_b))
    before = (node_ids[:, None] < node_ids[None, :]).astype(BF16)
    rank = jnp.dot(others.astype(BF16), before, preferred_element_type=F32) + 2.0
    at = jnp.where(others > 0.5, rank, jnp.where(own_two > 0.5, is_b.astype(F32), -1.0))
    listed = (at[:, :, None] == node_ids.astype(F32)[None, None, :]).astype(F32)
    nodes = jnp.sum(listed * node_ids.astype(F32)[None, :, None], axis=1).astype(jnp.int32)
    count = jnp.sum(others, axis=1).astype(jnp.int32) + 2
    table = jnp.concatenate(
        [jnp.broadcast_to(count[:, None], (8, 8)), nodes], axis=1
    ).reshape(-1)
    table = jnp.concatenate([jnp.broadcast_to(z, (8,)).astype(jnp.int32), table])
    vis = jnp.stack(
        [jnp.sum(listed * see_a[:, :, None], axis=1), jnp.sum(listed * see_b[:, :, None], axis=1)],
        axis=1,
    ).reshape(16, 64)
    grow = (node_ids[:, None] == jnp.arange(2048, dtype=jnp.int32)[None, :] // NODE).astype(BF16)
    seen = jnp.dot(vis.astype(BF16), grow, preferred_element_type=F32).reshape(8, 2, 2048)

    cosd, sind, table, seen = lax.optimization_barrier((cosd, sind, table, seen))
    kv, normed, meta_col = project_kv(
        (z // 2).reshape(1).astype(jnp.int32),
        xa,
        xb,
        input_gain.reshape(1, -1),
        w_keyval,
        cosd,
        sind,
        k_gain.reshape(1, -1),
    )
    kv_all = lax.all_to_all(kv, "y", 0, 0, tiled=True)
    normed, gate_up, down = lax.optimization_barrier((normed, w_gate_up[0], w_down[0]))
    gate_up_b = lax.ppermute(gate_up, "role", swap)
    down_b = lax.ppermute(down, "role", swap)
    q = project_q(normed, wq, cosd, sind, q_gain.reshape(1, -1))
    kv_all, gate_up_b, down_b = lax.optimization_barrier((kv_all, gate_up_b, down_b))
    partial = attend(table, q, kv_all, seen, wo).reshape(8, 64, 2048)
    attn = jnp.concatenate(
        [ring_scatter(partial[:, :, :half]), ring_scatter(partial[:, :, half:])], axis=1
    )
    middle = (own.astype(F32) + attn).astype(BF16)
    middle_f = middle.astype(F32)
    post_normed = rms_scale(middle_f, post_gain).astype(BF16)

    slots = 16 * CAP * N_Z
    spread, gate = route(place, meta_col, slots)
    pa = ring_gather(post_normed[:, :half])
    pb = ring_gather(post_normed[:, half:])
    outgoing = spread_rows(spread, pa, pb)
    received = lax.all_to_all(
        outgoing.reshape(16, CAP * N_Z, 2048), ("grp", "y"), 0, 0, tiled=True
    )
    result = ffn(received.reshape(slots, 2048), gate_up, gate_up_b, down, down_b)
    returned = lax.all_to_all(
        result.reshape(16, CAP * N_Z, 2048), ("grp", "y"), 0, 0, tiled=True
    )
    moe_part = combine(gate, returned.reshape(slots, 2048)).reshape(8, 64, 2048)
    moe = jnp.concatenate(
        [ring_scatter(moe_part[:, :, :half]), ring_scatter(moe_part[:, :, half:])], axis=1
    )
    return (middle_f + moe).astype(BF16)[None]


def solution(mesh):
    split = Mesh(mesh.devices.reshape(2, 4, 8, 4), ("role", "grp", "z", "y"))
    seq = ("z", "y")
    in_specs = (
        P(("role", "grp"), seq, None),
        P(("role", "grp"), None),
        P(("role", "grp"), seq, None),
        P(("role", "grp"), seq, None),
        P(),
        P(),
        P(),
        P(),
        P(None, seq),
        P(),
        P(seq, None),
        P(("grp", "z", "y"), None, None, "role"),
        P(("grp", "z", "y"), "role", None),
    )
    out_specs = P(("role", "grp"), seq, None)

    return jax.shard_map(body, mesh=split, in_specs=in_specs, out_specs=out_specs, check_vma=False)
```

```python
import math

import jax
import jax.numpy as jnp
from jax import lax
from jax.experimental import pallas as pl
from jax.experimental.pallas import tpu as pltpu
from jax.sharding import Mesh, PartitionSpec as P


NODE = 32
CAP = 6
EPSILON = 1e-06
ROPE_BASE = 1000000.0
MASKED = -1e30
BF16 = jnp.bfloat16
F32 = jnp.float32
N_Z = 8
N_Y = 4
CHUNK = 12
LISTED = 72
VMEM_LIMIT = 60 * 1024 * 1024


def shift(x, axis, size, by):
    return lax.ppermute(x, axis, [(i, (i + by) % size) for i in range(size)])


def ring_gather(x):
    fwd, bwd = [x], [x]
    for step in range(4):
        fwd.append(shift(fwd[-1], "z", N_Z, 1))
        if step < 3:
            bwd.append(shift(bwd[-1], "z", N_Z, N_Z - 1))
    return fwd + bwd[:0:-1]


def ring_scatter(slabs):
    def plus(a, b):
        return (a.astype(F32) + b.astype(F32)).astype(BF16)

    def ahead(cols):
        part = slabs[4, :, cols]
        for k in (5, 6, 7):
            part = plus(shift(part, "z", N_Z, 1), slabs[k, :, cols])
        return shift(part, "z", N_Z, 1)

    def back(cols):
        part = slabs[3, :, cols]
        for k in (2, 1):
            part = plus(shift(part, "z", N_Z, N_Z - 1), slabs[k, :, cols])
        return shift(part, "z", N_Z, N_Z - 1)

    fwd = [ahead(slice(0, 896)), ahead(slice(896, 2048))]
    bwd = [back(slice(0, 1280)), back(slice(1280, 2048))]
    fwd, bwd = jnp.concatenate(fwd, axis=1), jnp.concatenate(bwd, axis=1)
    return fwd.astype(F32) + bwd.astype(F32) + slabs[0].astype(F32)


def rms_scale(values, gain):
    mean_sq = jnp.mean(values * values, axis=-1, keepdims=True)
    return values * lax.rsqrt(mean_sq + EPSILON) * gain


def kv_kernel(kv_ref, *refs):
    pieces_a, pieces_b = refs[:N_Z], refs[N_Z : 2 * N_Z]
    gain, wkv, cosd, sind, kg, kv_out, n_out, meta_out = refs[2 * N_Z :]
    width = pieces_a[0].shape[1]
    for k in range(N_Z):
        rows = slice(k * 64, (k + 1) * 64)
        fa = pieces_a[k][...].astype(F32)
        fb = pieces_b[k][:, :width].astype(F32)
        mean_sq = (
            jnp.sum(fa * fa, axis=-1, keepdims=True) + jnp.sum(fb * fb, axis=-1, keepdims=True)
        ) / (2 * width)
        scale = lax.rsqrt(mean_sq + EPSILON)
        n_out[rows, :width] = (fa * scale * gain[:, :width]).astype(BF16)
        n_out[rows, width:] = (fb * scale * gain[:, width:]).astype(BF16)
        meta_out[rows] = pieces_b[k][:, width:]
    proj = jnp.dot(n_out[...], wkv[0], preferred_element_type=F32).astype(BF16)
    u = rms_scale(proj[:, :128].astype(F32), kg[...])
    keys = (u * cosd[...] + pltpu.roll(u, 64, 1) * sind[...]).astype(BF16)
    for copy in range(N_Y):
        kv_out[copy, :, :128] = keys
        kv_out[copy, :, 128:] = proj[:, 128:]


def project_kv(kv_index, xa, xb, gain, w_keyval, cosd, sind, k_gain):
    total = 64 * N_Z
    whole = lambda shape: pl.BlockSpec(shape, lambda i, s: (0,) * len(shape))
    return pl.pallas_call(
        kv_kernel,
        out_shape=(
            jax.ShapeDtypeStruct((N_Y, total, 256), BF16),
            jax.ShapeDtypeStruct((total, 2048), BF16),
            jax.ShapeDtypeStruct((total, 128), BF16),
        ),
        grid_spec=pltpu.PrefetchScalarGridSpec(
            num_scalar_prefetch=1,
            grid=(1,),
            in_specs=[whole(p.shape) for p in xa + xb]
            + [
                whole((1, 2048)),
                pl.BlockSpec((1, 2048, 256), lambda i, s: (s[0], 0, 0)),
                whole((total, 128)),
                whole((total, 128)),
                whole((1, 128)),
            ],
            out_specs=(
                whole((N_Y, total, 256)),
                whole((total, 2048)),
                whole((total, 128)),
            ),
        ),
        compiler_params=pltpu.CompilerParams(vmem_limit_bytes=VMEM_LIMIT),
        name="project_kv",
    )(kv_index, *xa, *xb, gain, w_keyval, cosd, sind, k_gain)


def q_kernel(n, wq0, wq1, wq2, wq3, cosd, sind, qg, q_out, w_scr):
    @pl.when(pl.program_id(0) == 0)
    def _():
        for h, w in enumerate((wq0, wq1, wq2, wq3)):
            w_scr[:, h * 128 : (h + 1) * 128] = w[...]

    proj = jnp.dot(n[...], w_scr[...], preferred_element_type=F32).astype(BF16)
    cos = cosd[...]
    sin = sind[...]
    for h in range(4):
        u = rms_scale(proj[:, h * 128 : (h + 1) * 128].astype(F32), qg[...])
        q_out[h] = (u * cos + pltpu.roll(u, 64, 1) * sin).astype(BF16)


def project_q(n, wq, cosd, sind, q_gain):
    rows = 256
    total = n.shape[0]
    whole = lambda shape: pl.BlockSpec(shape, lambda i: (0,) * len(shape))
    return pl.pallas_call(
        q_kernel,
        out_shape=jax.ShapeDtypeStruct((4, total, 128), BF16),
        grid=(total // rows,),
        in_specs=[pl.BlockSpec((rows, 2048), lambda i: (i, 0))]
        + [whole((2048, 128))] * 4
        + [
            pl.BlockSpec((rows, 128), lambda i: (i, 0)),
            pl.BlockSpec((rows, 128), lambda i: (i, 0)),
            whole((1, 128)),
        ],
        out_specs=pl.BlockSpec((4, rows, 128), lambda i: (0, i, 0)),
        scratch_shapes=[pltpu.VMEM((2048, 512), BF16)],
        compiler_params=pltpu.CompilerParams(vmem_limit_bytes=VMEM_LIMIT),
        name="project_q",
    )(n, *wq, cosd, sind, q_gain)


def attend_kernel(table, q, kv, seen, wo0, wo1, wo2, wo3, out, att, w_scr, kv_scr):
    step_id = pl.program_id(0)
    z = table[0]
    keys = CHUNK * NODE

    @pl.when(step_id == 0)
    def _():
        for h, w in enumerate((wo0, wo1, wo2, wo3)):
            w_scr[h * 128 : (h + 1) * 128] = w[...]

    inv_scale = 1.0 / math.sqrt(128)
    row = lax.broadcasted_iota(jnp.int32, (64, keys), 0)
    col = lax.broadcasted_iota(jnp.int32, (64, keys), 1)
    later = (col < 64) & (row // NODE == col // NODE) & (col > row)
    bases = [8 + (2 * step_id + b) * (8 + LISTED) for b in range(2)]
    queries = [q[:, b * 64 : (b + 1) * 64].reshape(256, 128) for b in range(2)]

    def load(b, chunk):
        for s in range(CHUNK):
            node = table[bases[b] + 8 + chunk * CHUNK + s]
            plane = lax.rem(z - node // 8 + N_Z, N_Z)
            start = pl.multiple_of(plane * 64 + (node % 2) * NODE, NODE)
            kv_scr[b, s * NODE : (s + 1) * NODE] = kv[(node % 8) // 2, pl.ds(start, NODE), :]
        cols = pl.ds(pl.multiple_of(chunk * keys, keys), keys)
        mask = jnp.where(row < NODE, seen[b, 0:1, cols], seen[b, 1:2, cols]) < 0.5
        scores = (
            lax.dot_general(
                queries[b],
                kv_scr[b, :, :128],
                (((1,), (1,)), ((), ())),
                preferred_element_type=F32,
            )
            * inv_scale
        )
        return scores.reshape(4, 64, keys), mask

    def weighed(b, probs):
        return jnp.dot(probs.astype(BF16), kv_scr[b, :, 128:], preferred_element_type=F32)

    firsts = [load(b, 0) for b in range(2)]
    scores = [
        jnp.where((mask | later)[None], MASKED, sc).reshape(256, keys) for sc, mask in firsts
    ]
    tops = [jnp.max(sc, axis=-1, keepdims=True) for sc in scores]
    probs = [jnp.exp(sc - top) for sc, top in zip(scores, tops)]
    totals = [jnp.sum(p, axis=-1, keepdims=True) for p in probs]
    mixes = [weighed(b, probs[b]) for b in range(2)]

    for b in range(2):

        def step(chunk, carry, b=b):
            top, total, mixed = carry
            scores, mask = load(b, chunk)
            scores = jnp.where(mask[None], MASKED, scores).reshape(256, keys)
            new_top = jnp.maximum(top, jnp.max(scores, axis=-1, keepdims=True))
            old = jnp.exp(top - new_top)
            probs = jnp.exp(scores - new_top)
            total = old * total + jnp.sum(probs, axis=-1, keepdims=True)
            return new_top, total, old * mixed + weighed(b, probs)

        chunks = (table[bases[b]] + CHUNK - 1) // CHUNK
        _, total, mixed = lax.fori_loop(1, chunks, step, (tops[b], totals[b], mixes[b]))
        attended = (mixed / total).astype(BF16)
        at = pl.multiple_of((2 * step_id + b) * 64, 64)
        for h in range(4):
            att[pl.ds(at, 64), h * 128 : (h + 1) * 128] = attended[h * 64 : (h + 1) * 64]

    @pl.when(step_id == N_Z // 2 - 1)
    def _():
        out[...] = jnp.dot(att[...], w_scr[...], preferred_element_type=F32).astype(BF16)


def attend(table, q, kv, seen, wo):
    whole = lambda shape: pl.BlockSpec(shape, lambda i, s: (0,) * len(shape))
    return pl.pallas_call(
        attend_kernel,
        out_shape=jax.ShapeDtypeStruct((512, 2048), BF16),
        grid_spec=pltpu.PrefetchScalarGridSpec(
            num_scalar_prefetch=1,
            grid=(N_Z // 2,),
            in_specs=[
                pl.BlockSpec((4, 128, 128), lambda i, s: (0, i, 0)),
                whole((N_Y, 512, 256)),
                pl.BlockSpec((2, 2, LISTED * NODE), lambda i, s: (i, 0, 0)),
                whole((128, 2048)),
                whole((128, 2048)),
                whole((128, 2048)),
                whole((128, 2048)),
            ],
            out_specs=whole((512, 2048)),
            scratch_shapes=[
                pltpu.VMEM((512, 512), BF16),
                pltpu.VMEM((512, 2048), BF16),
                pltpu.VMEM((2, CHUNK * NODE, 256), BF16),
            ],
        ),
        compiler_params=pltpu.CompilerParams(vmem_limit_bytes=VMEM_LIMIT),
        name="attend",
    )(table, q, kv, seen, *wo)


def route_kernel(place, meta, spread_out, gate_out):
    slots = spread_out.shape[0]
    rows = meta.shape[0]
    per = slots // 16
    z = place[0]
    info = meta[...].astype(F32)
    member = lax.broadcasted_iota(jnp.int32, (1, 128), 1)
    expert = (member // N_Y) * (N_Z * N_Y) + z * N_Y + member % N_Y
    expert = jnp.where(member < 16, expert, -1).astype(F32)
    hot = jnp.zeros((rows, 128), F32)
    high = jnp.zeros((rows, 128), F32)
    for i in range(8):
        same = info[:, i : i + 1] == expert
        hot = hot + jnp.where(same, 1.0, 0.0)
        high = high + jnp.where(same, info[:, 8 + i : 9 + i], 0.0)
    upto = lax.broadcasted_iota(jnp.int32, (rows, rows), 0) >= lax.broadcasted_iota(
        jnp.int32, (rows, rows), 1
    )
    count = jnp.dot(
        jnp.where(upto, 1.0, 0.0).astype(BF16), hot.astype(BF16), preferred_element_type=F32
    )
    rank = (count * hot).astype(BF16)
    slot_of = lax.broadcasted_iota(jnp.int32, (128, slots), 1) // per
    grow = jnp.where(
        slot_of == lax.broadcasted_iota(jnp.int32, (128, slots), 0), 1.0, 0.0
    ).astype(BF16)
    wide = jnp.dot(rank, grow, preferred_element_type=F32)
    nth = (lax.broadcasted_iota(jnp.int32, (1, slots), 1) % per + 1).astype(F32)
    at = wide == nth
    gate_out[...] = jnp.where(
        at, jnp.dot(high.astype(BF16), grow, preferred_element_type=F32), 0.0
    ).astype(BF16)
    spread_out[...] = jnp.where(at, 1.0, 0.0).T.astype(BF16)


def route(place, meta, slots):
    rows = meta.shape[0]
    whole = lambda shape: pl.BlockSpec(shape, lambda i, s: (0,) * len(shape))
    return pl.pallas_call(
        route_kernel,
        out_shape=(
            jax.ShapeDtypeStruct((slots, rows), BF16),
            jax.ShapeDtypeStruct((rows, slots), BF16),
        ),
        grid_spec=pltpu.PrefetchScalarGridSpec(
            num_scalar_prefetch=1,
            grid=(1,),
            in_specs=[whole(meta.shape)],
            out_specs=(whole((slots, rows)), whole((rows, slots))),
        ),
        compiler_params=pltpu.CompilerParams(vmem_limit_bytes=VMEM_LIMIT),
        name="route",
    )(place, meta)


def ffn_kernel(x, gu_hbm, d_hbm, out, gate_up, down, sems):
    copies = [
        pltpu.make_async_copy(gu_hbm.at[0], gate_up.at[0], sems.at[0]),
        pltpu.make_async_copy(gu_hbm.at[1], gate_up.at[1], sems.at[1]),
        pltpu.make_async_copy(d_hbm, down, sems.at[2]),
    ]
    first = pl.program_id(0) == 0

    @pl.when(first)
    def _():
        for c in copies:
            c.start()
        copies[0].wait()

    rows = x[...]
    gate = jnp.dot(rows, gate_up[0], preferred_element_type=F32)

    @pl.when(first)
    def _():
        copies[1].wait()

    up = jnp.dot(rows, gate_up[1], preferred_element_type=F32)
    hidden = (gate / (1.0 + jnp.exp(-gate)) * up).astype(BF16)

    @pl.when(first)
    def _():
        copies[2].wait()

    out[...] = jnp.dot(hidden, down[...], preferred_element_type=F32).astype(BF16)


def ffn(x, gate_up, down):
    rows = 256
    width = x.shape[1]
    there = pl.BlockSpec(memory_space=pl.ANY)
    return pl.pallas_call(
        ffn_kernel,
        out_shape=jax.ShapeDtypeStruct(x.shape, BF16),
        grid=(x.shape[0] // rows,),
        in_specs=[pl.BlockSpec((rows, width), lambda i: (i, 0)), there, there],
        out_specs=pl.BlockSpec((rows, width), lambda i: (i, 0)),
        scratch_shapes=[
            pltpu.VMEM(gate_up.shape, BF16),
            pltpu.VMEM(down.shape, BF16),
            pltpu.SemaphoreType.DMA((3,)),
        ],
        compiler_params=pltpu.CompilerParams(vmem_limit_bytes=VMEM_LIMIT),
        name="ffn",
    )(x, gate_up, down)


def spread_kernel(*refs):
    pieces_a, pieces_b = refs[:N_Z], refs[N_Z : 2 * N_Z]
    spread, out, rows = refs[2 * N_Z :]
    width = pieces_a[0].shape[1]

    @pl.when(pl.program_id(0) == 0)
    def _():
        for k in range(N_Z):
            rows[k * 64 : (k + 1) * 64, :width] = pieces_a[k][...]
            rows[k * 64 : (k + 1) * 64, width:] = pieces_b[k][...]

    out[...] = jnp.dot(spread[...], rows[...], preferred_element_type=F32).astype(BF16)


def spread_rows(spread, pa, pb):
    width = 2 * pa[0].shape[1]
    slots, tokens = spread.shape
    whole = lambda shape: pl.BlockSpec(shape, lambda i: (0,) * len(shape))
    return pl.pallas_call(
        spread_kernel,
        out_shape=jax.ShapeDtypeStruct((slots, width), BF16),
        grid=(slots // 256,),
        in_specs=[whole(p.shape) for p in pa + pb]
        + [pl.BlockSpec((256, tokens), lambda i: (i, 0))],
        out_specs=pl.BlockSpec((256, width), lambda i: (i, 0)),
        scratch_shapes=[pltpu.VMEM((tokens, width), BF16)],
        compiler_params=pltpu.CompilerParams(vmem_limit_bytes=VMEM_LIMIT),
        name="spread",
    )(*pa, *pb, spread)


def combine_kernel(g, r, out):
    out[...] = jnp.dot(g[...], r[...], preferred_element_type=F32).astype(BF16)


def combine(g, r):
    rows = 256
    return pl.pallas_call(
        combine_kernel,
        out_shape=jax.ShapeDtypeStruct((g.shape[0], r.shape[1]), BF16),
        grid=(g.shape[0] // rows,),
        in_specs=[
            pl.BlockSpec((rows, g.shape[1]), lambda i: (i, 0)),
            pl.BlockSpec(r.shape, lambda i: (0, 0)),
        ],
        out_specs=pl.BlockSpec((rows, r.shape[1]), lambda i: (i, 0)),
        compiler_params=pltpu.CompilerParams(vmem_limit_bytes=VMEM_LIMIT),
        name="combine",
    )(g, r)


def ancestry(parent_row):
    nodes = parent_row.shape[0]
    ids = jnp.arange(nodes, dtype=jnp.int32)
    reach = ((parent_row[:, None] == ids[None, :]) | (ids[:, None] == ids[None, :])).astype(BF16)
    for _ in range((nodes - 1).bit_length()):
        reach = (jnp.dot(reach, reach, preferred_element_type=F32) > 0.5).astype(BF16)
    return reach


def body(
    tokens,
    parents,
    route_ids,
    route_gates,
    input_gain,
    q_gain,
    k_gain,
    post_gain,
    w_query,
    w_keyval,
    w_out,
    w_gate_up,
    w_down,
):
    z = lax.axis_index("z")
    y = lax.axis_index("y")
    place = jnp.stack([z, y]).astype(jnp.int32)
    half = 1024
    swap = [(0, 1), (1, 0)]

    meta = jnp.concatenate(
        [route_ids[0].astype(BF16), route_gates[0].astype(BF16), jnp.zeros((64, 112), BF16)], axis=1
    )
    own = tokens[0]
    xa = ring_gather(own[:, :half])
    xb = ring_gather(jnp.concatenate([own[:, half:], meta], axis=1))
    wq = [w_query] + [shift(w_query, "y", N_Y, k) for k in (1, 3, 2)]
    wo = [w_out] + [shift(w_out, "y", N_Y, k) for k in (1, 3, 2)]

    reach = ancestry(parents[0])
    depth = jnp.sum(reach.astype(F32), axis=1) - 1.0
    node_ids = jnp.arange(64, dtype=jnp.int32)
    t512 = jnp.arange(512, dtype=jnp.int32)
    node_of = ((z - t512 // 64) % N_Z) * 8 + y * 2 + (t512 % 64) // NODE
    depth_of = jnp.sum(
        jnp.where(node_of[:, None] == node_ids[None, :], depth[None, :], 0.0), axis=1
    )
    positions = depth_of * NODE + (t512 % NODE).astype(F32)
    frequency = jnp.power(ROPE_BASE, -2.0 * jnp.arange(64, dtype=F32) / 128)
    angles = positions[:, None] * frequency[None, :]
    cosine = jnp.cos(angles)
    sine = jnp.sin(angles)
    cosd = jnp.concatenate([cosine, cosine], axis=1)
    sind = jnp.concatenate([-sine, sine], axis=1)

    first = ((z - jnp.arange(8, dtype=jnp.int32)) % N_Z) * 8 + y * 2
    is_a = (first[:, None] == node_ids[None, :]).astype(BF16)
    is_b = (first[:, None] + 1 == node_ids[None, :]).astype(BF16)
    see_a = jnp.dot(is_a, reach, preferred_element_type=F32)
    see_b = jnp.dot(is_b, reach, preferred_element_type=F32)
    own_two = (is_a + is_b).astype(F32)
    others = jnp.where(own_two > 0.5, 0.0, jnp.maximum(see_a, see_b))
    before = (node_ids[:, None] < node_ids[None, :]).astype(BF16)
    rank = jnp.dot(others.astype(BF16), before, preferred_element_type=F32) + 2.0
    at = jnp.where(others > 0.5, rank, jnp.where(own_two > 0.5, is_b.astype(F32), -1.0))
    spots = jnp.arange(LISTED, dtype=jnp.int32)
    listed = (at[:, :, None] == spots.astype(F32)[None, None, :]).astype(F32)
    nodes = jnp.sum(listed * node_ids.astype(F32)[None, :, None], axis=1).astype(jnp.int32)
    count = jnp.sum(others, axis=1).astype(jnp.int32) + 2
    table = jnp.concatenate(
        [jnp.broadcast_to(count[:, None], (8, 8)), nodes], axis=1
    ).reshape(-1)
    table = jnp.concatenate([jnp.broadcast_to(z, (8,)).astype(jnp.int32), table])
    vis = jnp.stack(
        [jnp.sum(listed * see_a[:, :, None], axis=1), jnp.sum(listed * see_b[:, :, None], axis=1)],
        axis=1,
    ).reshape(16, LISTED)
    wide = jnp.arange(LISTED * NODE, dtype=jnp.int32)
    grow = (spots[:, None] == wide[None, :] // NODE).astype(BF16)
    seen = jnp.dot(vis.astype(BF16), grow, preferred_element_type=F32)
    seen = seen.reshape(8, 2, LISTED * NODE)

    cosd, sind, table, seen = lax.optimization_barrier((cosd, sind, table, seen))
    kv, normed, meta_col = project_kv(
        (z // 2).reshape(1).astype(jnp.int32),
        xa,
        xb,
        input_gain.reshape(1, -1),
        w_keyval,
        cosd,
        sind,
        k_gain.reshape(1, -1),
    )
    kv_all = lax.all_to_all(kv, "y", 0, 0, tiled=True)
    normed, gate_up, down = lax.optimization_barrier((normed, w_gate_up[0], w_down[0]))
    gate_up_b = lax.ppermute(gate_up, "role", swap)
    down_b = lax.ppermute(down, "role", swap)
    q = project_q(normed, wq, cosd, sind, q_gain.reshape(1, -1))
    slots = 16 * CAP * N_Z
    spread, gate = route(place, meta_col, slots)
    kv_all, gate_up_b, down_b, spread, gate = lax.optimization_barrier(
        (kv_all, gate_up_b, down_b, spread, gate)
    )
    partial = attend(table, q, kv_all, seen, wo).reshape(8, 64, 2048)
    attn = ring_scatter(partial)
    middle = (own.astype(F32) + attn).astype(BF16)
    middle_f = middle.astype(F32)
    post_normed = rms_scale(middle_f, post_gain).astype(BF16)

    pa = ring_gather(post_normed[:, :half])
    pb = ring_gather(post_normed[:, half:])
    outgoing = spread_rows(spread, pa, pb)
    outgoing, gate_up_b, down_b = lax.optimization_barrier((outgoing, gate_up_b, down_b))
    received = lax.all_to_all(
        outgoing.reshape(16, CAP * N_Z, 2048), ("grp", "y"), 0, 0, tiled=True
    )
    gate_up = jnp.concatenate([gate_up, gate_up_b], axis=2)
    down = jnp.concatenate([down, down_b], axis=0)
    result = ffn(received.reshape(slots, 2048), gate_up, down)
    returned = lax.all_to_all(
        result.reshape(16, CAP * N_Z, 2048), ("grp", "y"), 0, 0, tiled=True
    )
    moe_part = combine(gate, returned.reshape(slots, 2048)).reshape(8, 64, 2048)
    moe = ring_scatter(moe_part)
    return (middle_f + moe).astype(BF16)[None]


def solution(mesh):
    split = Mesh(mesh.devices.reshape(2, 4, 8, 4), ("role", "grp", "z", "y"))
    seq = ("z", "y")
    in_specs = (
        P(("role", "grp"), seq, None),
        P(("role", "grp"), None),
        P(("role", "grp"), seq, None),
        P(("role", "grp"), seq, None),
        P(),
        P(),
        P(),
        P(),
        P(None, seq),
        P(),
        P(seq, None),
        P(("grp", "z", "y"), None, None, "role"),
        P(("grp", "z", "y"), "role", None),
    )
    out_specs = P(("role", "grp"), seq, None)

    return jax.shard_map(body, mesh=split, in_specs=in_specs, out_specs=out_specs, check_vma=False)
```

```python
import math

import jax
import jax.numpy as jnp
from jax import lax
from jax.experimental import pallas as pl
from jax.experimental.pallas import tpu as pltpu
from jax.sharding import Mesh, PartitionSpec as P


NODE = 32
CAP = 6
EPSILON = 1e-06
ROPE_BASE = 1000000.0
MASKED = -1e30
BF16 = jnp.bfloat16
F32 = jnp.float32
N_Z = 8
N_Y = 4
CHUNK = 12
LISTED = 72
VMEM_LIMIT = 20 * 1024 * 1024
SPLIT_AHEAD = 896
SPLIT_BACK = 1280


def shift(x, axis, size, by):
    return lax.ppermute(x, axis, [(i, (i + by) % size) for i in range(size)])


def ring_gather(x):
    fwd, bwd = [x], [x]
    for step in range(4):
        fwd.append(shift(fwd[-1], "z", N_Z, 1))
        if step < 3:
            bwd.append(shift(bwd[-1], "z", N_Z, N_Z - 1))
    return fwd + bwd[:0:-1]


def ring_scatter(slabs, firsts):
    def plus(a, b):
        return (a.astype(F32) + b.astype(F32)).astype(BF16)

    def ahead(part, cols):
        for k in (5, 6, 7):
            part = plus(shift(part, "z", N_Z, 1), slabs[k, :, cols])
        return shift(part, "z", N_Z, 1)

    def back(part, cols):
        for k in (2, 1):
            part = plus(shift(part, "z", N_Z, N_Z - 1), slabs[k, :, cols])
        return shift(part, "z", N_Z, N_Z - 1)

    fwd = [
        ahead(firsts[0], slice(0, SPLIT_AHEAD)),
        ahead(firsts[1], slice(SPLIT_AHEAD, 2048)),
    ]
    bwd = [back(firsts[2], slice(0, SPLIT_BACK)), back(firsts[3], slice(SPLIT_BACK, 2048))]
    fwd, bwd = jnp.concatenate(fwd, axis=1), jnp.concatenate(bwd, axis=1)
    return fwd.astype(F32) + bwd.astype(F32) + slabs[0].astype(F32)


FIRST_SHAPES = tuple(
    jax.ShapeDtypeStruct((64, w), BF16)
    for w in (SPLIT_AHEAD, 2048 - SPLIT_AHEAD, SPLIT_BACK, 2048 - SPLIT_BACK)
)


def resident():
    return pl.BlockSpec(memory_space=pltpu.VMEM)


def rms_scale(values, gain):
    mean_sq = jnp.mean(values * values, axis=-1, keepdims=True)
    return values * lax.rsqrt(mean_sq + EPSILON) * gain


def kv_kernel(kv_ref, *refs):
    pieces_a, pieces_b = refs[:N_Z], refs[N_Z : 2 * N_Z]
    gain, w_all, cosd, sind, kg, kv_out, n_out, meta_out, wkv, sem = refs[2 * N_Z :]
    fetch = pltpu.make_async_copy(w_all.at[kv_ref[0]], wkv, sem)
    fetch.start()
    width = pieces_a[0].shape[1]
    for k in range(N_Z):
        rows = slice(k * 64, (k + 1) * 64)
        fa = pieces_a[k][...].astype(F32)
        fb = pieces_b[k][:, :width].astype(F32)
        mean_sq = (
            jnp.sum(fa * fa, axis=-1, keepdims=True) + jnp.sum(fb * fb, axis=-1, keepdims=True)
        ) / (2 * width)
        scale = lax.rsqrt(mean_sq + EPSILON)
        n_out[rows, :width] = (fa * scale * gain[:, :width]).astype(BF16)
        n_out[rows, width:] = (fb * scale * gain[:, width:]).astype(BF16)
        meta_out[rows] = pieces_b[k][:, width:]
    fetch.wait()
    proj = jnp.dot(n_out[...], wkv[...], preferred_element_type=F32).astype(BF16)
    u = rms_scale(proj[:, :128].astype(F32), kg[...])
    keys = (u * cosd[...] + pltpu.roll(u, 64, 1) * sind[...]).astype(BF16)
    for copy in range(N_Y):
        kv_out[copy, :, :128] = keys
        kv_out[copy, :, 128:] = proj[:, 128:]


def project_kv(kv_index, xa, xb, gain, w_keyval, cosd, sind, k_gain):
    total = 64 * N_Z
    whole = lambda shape: pl.BlockSpec(shape, lambda i, s: (0,) * len(shape))
    return pl.pallas_call(
        kv_kernel,
        out_shape=(
            jax.ShapeDtypeStruct((N_Y, total, 256), BF16),
            jax.ShapeDtypeStruct((total, 2048), BF16),
            jax.ShapeDtypeStruct((total, 128), BF16),
        ),
        grid_spec=pltpu.PrefetchScalarGridSpec(
            num_scalar_prefetch=1,
            grid=(1,),
            in_specs=[resident() for p in xa + xb]
            + [
                whole((1, 2048)),
                pl.BlockSpec(memory_space=pltpu.HBM),
                whole((total, 128)),
                whole((total, 128)),
                whole((1, 128)),
            ],
            out_specs=(
                whole((N_Y, total, 256)),
                whole((total, 2048)),
                whole((total, 128)),
            ),
            scratch_shapes=[pltpu.VMEM((2048, 256), BF16), pltpu.SemaphoreType.DMA],
        ),
        compiler_params=pltpu.CompilerParams(vmem_limit_bytes=VMEM_LIMIT),
        name="project_kv",
    )(kv_index, *xa, *xb, gain, w_keyval, cosd, sind, k_gain)


def q_kernel(n, wq0, wq1, wq2, wq3, cosd, sind, qg, q_out, w_scr):
    @pl.when(pl.program_id(0) == 0)
    def _():
        for h, w in enumerate((wq0, wq1, wq2, wq3)):
            w_scr[:, h * 128 : (h + 1) * 128] = w[...]

    proj = jnp.dot(n[...], w_scr[...], preferred_element_type=F32).astype(BF16)
    cos = cosd[...]
    sin = sind[...]
    for h in range(4):
        u = rms_scale(proj[:, h * 128 : (h + 1) * 128].astype(F32), qg[...])
        q_out[h] = (u * cos + pltpu.roll(u, 64, 1) * sin).astype(BF16)


def project_q(n, wq, cosd, sind, q_gain):
    rows = 256
    total = n.shape[0]
    whole = lambda shape: pl.BlockSpec(shape, lambda i: (0,) * len(shape))
    return pl.pallas_call(
        q_kernel,
        out_shape=jax.ShapeDtypeStruct((4, total, 128), BF16),
        grid=(total // rows,),
        in_specs=[pl.BlockSpec((rows, 2048), lambda i: (i, 0))]
        + [resident()] * 4
        + [
            pl.BlockSpec((rows, 128), lambda i: (i, 0)),
            pl.BlockSpec((rows, 128), lambda i: (i, 0)),
            whole((1, 128)),
        ],
        out_specs=pl.BlockSpec((4, rows, 128), lambda i: (0, i, 0)),
        scratch_shapes=[pltpu.VMEM((2048, 512), BF16)],
        compiler_params=pltpu.CompilerParams(vmem_limit_bytes=VMEM_LIMIT),
        name="project_q",
    )(n, *wq, cosd, sind, q_gain)


def attend_kernel(
    table, q, kv, seen, wo0, wo1, wo2, wo3, out, fa, fb, ba, bb, att, w_scr, kv_scr
):
    step_id = pl.program_id(0)
    z = table[0]
    keys = CHUNK * NODE

    @pl.when(step_id == 0)
    def _():
        for h, w in enumerate((wo0, wo1, wo2, wo3)):
            w_scr[h * 128 : (h + 1) * 128] = w[...]

    inv_scale = 1.0 / math.sqrt(128)
    row = lax.broadcasted_iota(jnp.int32, (64, keys), 0)
    col = lax.broadcasted_iota(jnp.int32, (64, keys), 1)
    later = (col < 64) & (row // NODE == col // NODE) & (col > row)
    bases = [8 + (2 * step_id + b) * (8 + LISTED) for b in range(2)]
    queries = [q[:, b * 64 : (b + 1) * 64].reshape(256, 128) for b in range(2)]

    def load(b, chunk):
        for s in range(CHUNK):
            node = table[bases[b] + 8 + chunk * CHUNK + s]
            plane = lax.rem(z - node // 8 + N_Z, N_Z)
            start = pl.multiple_of(plane * 64 + (node % 2) * NODE, NODE)
            kv_scr[b, s * NODE : (s + 1) * NODE] = kv[(node % 8) // 2, pl.ds(start, NODE), :]
        cols = pl.ds(pl.multiple_of(chunk * keys, keys), keys)
        mask = jnp.where(row < NODE, seen[b, 0:1, cols], seen[b, 1:2, cols]) < 0.5
        scores = (
            lax.dot_general(
                queries[b],
                kv_scr[b, :, :128],
                (((1,), (1,)), ((), ())),
                preferred_element_type=F32,
            )
            * inv_scale
        )
        return scores.reshape(4, 64, keys), mask

    def weighed(b, probs):
        return jnp.dot(probs.astype(BF16), kv_scr[b, :, 128:], preferred_element_type=F32)

    firsts = [load(b, 0) for b in range(2)]
    scores = [
        jnp.where((mask | later)[None], MASKED, sc).reshape(256, keys) for sc, mask in firsts
    ]
    tops = [jnp.max(sc, axis=-1, keepdims=True) for sc in scores]
    probs = [jnp.exp(sc - top) for sc, top in zip(scores, tops)]
    totals = [jnp.sum(p, axis=-1, keepdims=True) for p in probs]
    mixes = [weighed(b, probs[b]) for b in range(2)]

    for b in range(2):

        def step(chunk, carry, b=b):
            top, total, mixed = carry
            scores, mask = load(b, chunk)
            scores = jnp.where(mask[None], MASKED, scores).reshape(256, keys)
            new_top = jnp.maximum(top, jnp.max(scores, axis=-1, keepdims=True))
            old = jnp.exp(top - new_top)
            probs = jnp.exp(scores - new_top)
            total = old * total + jnp.sum(probs, axis=-1, keepdims=True)
            return new_top, total, old * mixed + weighed(b, probs)

        chunks = (table[bases[b]] + CHUNK - 1) // CHUNK
        _, total, mixed = lax.fori_loop(1, chunks, step, (tops[b], totals[b], mixes[b]))
        attended = (mixed / total).astype(BF16)
        at = pl.multiple_of((2 * step_id + b) * 64, 64)
        for h in range(4):
            att[pl.ds(at, 64), h * 128 : (h + 1) * 128] = attended[h * 64 : (h + 1) * 64]

    @pl.when(step_id == N_Z // 2 - 1)
    def _():
        full = jnp.dot(att[...], w_scr[...], preferred_element_type=F32).astype(BF16)
        out[...] = full
        fa[...] = full[256:320, :SPLIT_AHEAD]
        fb[...] = full[256:320, SPLIT_AHEAD:]
        ba[...] = full[192:256, :SPLIT_BACK]
        bb[...] = full[192:256, SPLIT_BACK:]


def attend(table, q, kv, seen, wo):
    whole = lambda shape: pl.BlockSpec(shape, lambda i, s: (0,) * len(shape))
    return pl.pallas_call(
        attend_kernel,
        out_shape=(jax.ShapeDtypeStruct((512, 2048), BF16),) + FIRST_SHAPES,
        grid_spec=pltpu.PrefetchScalarGridSpec(
            num_scalar_prefetch=1,
            grid=(N_Z // 2,),
            in_specs=[
                pl.BlockSpec((4, 128, 128), lambda i, s: (0, i, 0)),
                resident(),
                pl.BlockSpec((2, 2, LISTED * NODE), lambda i, s: (i, 0, 0)),
                resident(),
                resident(),
                resident(),
                resident(),
            ],
            out_specs=(whole((512, 2048)),) + tuple(whole(f.shape) for f in FIRST_SHAPES),
            scratch_shapes=[
                pltpu.VMEM((512, 512), BF16),
                pltpu.VMEM((512, 2048), BF16),
                pltpu.VMEM((2, CHUNK * NODE, 256), BF16),
            ],
        ),
        compiler_params=pltpu.CompilerParams(vmem_limit_bytes=VMEM_LIMIT),
        name="attend",
    )(table, q, kv, seen, *wo)


def route_kernel(place, meta, spread_out, gate_out):
    slots = spread_out.shape[0]
    rows = meta.shape[0]
    per = slots // 16
    z = place[0]
    info = meta[...].astype(F32)
    member = lax.broadcasted_iota(jnp.int32, (1, 128), 1)
    expert = (member // N_Y) * (N_Z * N_Y) + z * N_Y + member % N_Y
    expert = jnp.where(member < 16, expert, -1).astype(F32)
    hot = jnp.zeros((rows, 128), F32)
    high = jnp.zeros((rows, 128), F32)
    for i in range(8):
        same = info[:, i : i + 1] == expert
        hot = hot + jnp.where(same, 1.0, 0.0)
        high = high + jnp.where(same, info[:, 8 + i : 9 + i], 0.0)
    upto = lax.broadcasted_iota(jnp.int32, (rows, rows), 0) >= lax.broadcasted_iota(
        jnp.int32, (rows, rows), 1
    )
    count = jnp.dot(
        jnp.where(upto, 1.0, 0.0).astype(BF16), hot.astype(BF16), preferred_element_type=F32
    )
    rank = (count * hot).astype(BF16)
    slot_of = lax.broadcasted_iota(jnp.int32, (128, slots), 1) // per
    grow = jnp.where(
        slot_of == lax.broadcasted_iota(jnp.int32, (128, slots), 0), 1.0, 0.0
    ).astype(BF16)
    wide = jnp.dot(rank, grow, preferred_element_type=F32)
    nth = (lax.broadcasted_iota(jnp.int32, (1, slots), 1) % per + 1).astype(F32)
    at = wide == nth
    gate_out[...] = jnp.where(
        at, jnp.dot(high.astype(BF16), grow, preferred_element_type=F32), 0.0
    ).astype(BF16)
    spread_out[...] = jnp.where(at, 1.0, 0.0).T.astype(BF16)


def route(place, meta, slots):
    rows = meta.shape[0]
    whole = lambda shape: pl.BlockSpec(shape, lambda i, s: (0,) * len(shape))
    return pl.pallas_call(
        route_kernel,
        out_shape=(
            jax.ShapeDtypeStruct((slots, rows), BF16),
            jax.ShapeDtypeStruct((rows, slots), BF16),
        ),
        grid_spec=pltpu.PrefetchScalarGridSpec(
            num_scalar_prefetch=1,
            grid=(1,),
            in_specs=[whole(meta.shape)],
            out_specs=(whole((slots, rows)), whole((rows, slots))),
        ),
        compiler_params=pltpu.CompilerParams(vmem_limit_bytes=VMEM_LIMIT),
        name="route",
    )(place, meta)


def ffn_kernel(x, gate_up, down, out):
    rows = x[...]
    gate = jnp.dot(rows, gate_up[0], preferred_element_type=F32)
    up = jnp.dot(rows, gate_up[1], preferred_element_type=F32)
    hidden = (gate / (1.0 + jnp.exp(-gate)) * up).astype(BF16)
    out[...] = jnp.dot(hidden, down[...], preferred_element_type=F32).astype(BF16)


def ffn(x, gate_up, down):
    rows = 256
    width = x.shape[1]
    return pl.pallas_call(
        ffn_kernel,
        out_shape=jax.ShapeDtypeStruct(x.shape, BF16),
        grid=(x.shape[0] // rows,),
        in_specs=[pl.BlockSpec((rows, width), lambda i: (i, 0)), resident(), resident()],
        out_specs=pl.BlockSpec((rows, width), lambda i: (i, 0)),
        compiler_params=pltpu.CompilerParams(vmem_limit_bytes=VMEM_LIMIT),
        name="ffn",
    )(x, gate_up, down)


def spread_kernel(*refs):
    pieces_a, pieces_b = refs[:N_Z], refs[N_Z : 2 * N_Z]
    spread, out, rows = refs[2 * N_Z :]
    width = pieces_a[0].shape[1]

    @pl.when(pl.program_id(0) == 0)
    def _():
        for k in range(N_Z):
            rows[k * 64 : (k + 1) * 64, :width] = pieces_a[k][...]
            rows[k * 64 : (k + 1) * 64, width:] = pieces_b[k][...]

    out[...] = jnp.dot(spread[...], rows[...], preferred_element_type=F32).astype(BF16)


def spread_rows(spread, pa, pb):
    width = 2 * pa[0].shape[1]
    slots, tokens = spread.shape
    return pl.pallas_call(
        spread_kernel,
        out_shape=jax.ShapeDtypeStruct((slots, width), BF16),
        grid=(slots // 256,),
        in_specs=[resident() for p in pa + pb]
        + [pl.BlockSpec((256, tokens), lambda i: (i, 0))],
        out_specs=pl.BlockSpec((256, width), lambda i: (i, 0)),
        scratch_shapes=[pltpu.VMEM((tokens, width), BF16)],
        compiler_params=pltpu.CompilerParams(vmem_limit_bytes=VMEM_LIMIT),
        name="spread",
    )(*pa, *pb, spread)


def combine_kernel(g, r, out, fa, fb, ba, bb):
    full = jnp.dot(g[...], r[...], preferred_element_type=F32).astype(BF16)
    out[...] = full

    @pl.when(pl.program_id(0) == 0)
    def _():
        ba[...] = full[192:256, :SPLIT_BACK]
        bb[...] = full[192:256, SPLIT_BACK:]

    @pl.when(pl.program_id(0) == 1)
    def _():
        fa[...] = full[:64, :SPLIT_AHEAD]
        fb[...] = full[:64, SPLIT_AHEAD:]


def combine(g, r):
    rows = 256
    return pl.pallas_call(
        combine_kernel,
        out_shape=(jax.ShapeDtypeStruct((g.shape[0], r.shape[1]), BF16),) + FIRST_SHAPES,
        grid=(g.shape[0] // rows,),
        in_specs=[pl.BlockSpec((rows, g.shape[1]), lambda i: (i, 0)), resident()],
        out_specs=(pl.BlockSpec((rows, r.shape[1]), lambda i: (i, 0)),)
        + tuple(pl.BlockSpec(f.shape, lambda i: (0, 0)) for f in FIRST_SHAPES),
        compiler_params=pltpu.CompilerParams(vmem_limit_bytes=VMEM_LIMIT),
        name="combine",
    )(g, r)


def ancestry(parent_row):
    nodes = parent_row.shape[0]
    ids = jnp.arange(nodes, dtype=jnp.int32)
    reach = ((parent_row[:, None] == ids[None, :]) | (ids[:, None] == ids[None, :])).astype(BF16)
    for _ in range((nodes - 1).bit_length()):
        reach = (jnp.dot(reach, reach, preferred_element_type=F32) > 0.5).astype(BF16)
    return reach


def body(
    tokens,
    parents,
    route_ids,
    route_gates,
    input_gain,
    q_gain,
    k_gain,
    post_gain,
    w_query,
    w_keyval,
    w_out,
    w_gate_up,
    w_down,
):
    z = lax.axis_index("z")
    y = lax.axis_index("y")
    place = jnp.stack([z, y]).astype(jnp.int32)
    half = 1024
    swap = [(0, 1), (1, 0)]

    meta = jnp.concatenate(
        [route_ids[0].astype(BF16), route_gates[0].astype(BF16), jnp.zeros((64, 112), BF16)], axis=1
    )
    own = tokens[0]
    xa = ring_gather(own[:, :half])
    xb = ring_gather(jnp.concatenate([own[:, half:], meta], axis=1))
    wq = [w_query] + [shift(w_query, "y", N_Y, k) for k in (1, 3, 2)]
    wo = [w_out] + [shift(w_out, "y", N_Y, k) for k in (1, 3, 2)]

    reach = ancestry(parents[0])
    depth = jnp.sum(reach.astype(F32), axis=1) - 1.0
    node_ids = jnp.arange(64, dtype=jnp.int32)
    t512 = jnp.arange(512, dtype=jnp.int32)
    node_of = ((z - t512 // 64) % N_Z) * 8 + y * 2 + (t512 % 64) // NODE
    depth_of = jnp.sum(
        jnp.where(node_of[:, None] == node_ids[None, :], depth[None, :], 0.0), axis=1
    )
    positions = depth_of * NODE + (t512 % NODE).astype(F32)
    frequency = jnp.power(ROPE_BASE, -2.0 * jnp.arange(64, dtype=F32) / 128)
    angles = positions[:, None] * frequency[None, :]
    cosine = jnp.cos(angles)
    sine = jnp.sin(angles)
    cosd = jnp.concatenate([cosine, cosine], axis=1)
    sind = jnp.concatenate([-sine, sine], axis=1)

    first = ((z - jnp.arange(8, dtype=jnp.int32)) % N_Z) * 8 + y * 2
    is_a = (first[:, None] == node_ids[None, :]).astype(BF16)
    is_b = (first[:, None] + 1 == node_ids[None, :]).astype(BF16)
    see_a = jnp.dot(is_a, reach, preferred_element_type=F32)
    see_b = jnp.dot(is_b, reach, preferred_element_type=F32)
    own_two = (is_a + is_b).astype(F32)
    others = jnp.where(own_two > 0.5, 0.0, jnp.maximum(see_a, see_b))
    before = (node_ids[:, None] < node_ids[None, :]).astype(BF16)
    rank = jnp.dot(others.astype(BF16), before, preferred_element_type=F32) + 2.0
    at = jnp.where(others > 0.5, rank, jnp.where(own_two > 0.5, is_b.astype(F32), -1.0))
    spots = jnp.arange(LISTED, dtype=jnp.int32)
    listed = (at[:, :, None] == spots.astype(F32)[None, None, :]).astype(F32)
    nodes = jnp.sum(listed * node_ids.astype(F32)[None, :, None], axis=1).astype(jnp.int32)
    count = jnp.sum(others, axis=1).astype(jnp.int32) + 2
    table = jnp.concatenate(
        [jnp.broadcast_to(count[:, None], (8, 8)), nodes], axis=1
    ).reshape(-1)
    table = jnp.concatenate([jnp.broadcast_to(z, (8,)).astype(jnp.int32), table])
    vis = jnp.stack(
        [jnp.sum(listed * see_a[:, :, None], axis=1), jnp.sum(listed * see_b[:, :, None], axis=1)],
        axis=1,
    ).reshape(16, LISTED)
    wide = jnp.arange(LISTED * NODE, dtype=jnp.int32)
    grow = (spots[:, None] == wide[None, :] // NODE).astype(BF16)
    seen = jnp.dot(vis.astype(BF16), grow, preferred_element_type=F32)
    seen = seen.reshape(8, 2, LISTED * NODE)

    cosd, sind, table, seen = lax.optimization_barrier((cosd, sind, table, seen))
    kv, normed, meta_col = project_kv(
        (z // 2).reshape(1).astype(jnp.int32),
        xa,
        xb,
        input_gain.reshape(1, -1),
        w_keyval,
        cosd,
        sind,
        k_gain.reshape(1, -1),
    )
    kv_all = lax.all_to_all(kv, "y", 0, 0, tiled=True)
    q = project_q(normed, wq, cosd, sind, q_gain.reshape(1, -1))
    slots = 16 * CAP * N_Z
    spread, gate = route(place, meta_col, slots)
    kv_all, spread, gate, gate_up, down = lax.optimization_barrier(
        (kv_all, spread, gate, w_gate_up[0], w_down[0])
    )
    gate_up_b = lax.ppermute(gate_up, "role", swap)
    down_b = lax.ppermute(down, "role", swap)
    partial, *firsts = attend(table, q, kv_all, seen, wo)
    attn = ring_scatter(partial.reshape(8, 64, 2048), firsts)
    middle = (own.astype(F32) + attn).astype(BF16)
    middle_f = middle.astype(F32)
    post_normed = rms_scale(middle_f, post_gain).astype(BF16)

    pa = ring_gather(post_normed[:, :half])
    pb = ring_gather(post_normed[:, half:])
    outgoing = spread_rows(spread, pa, pb)
    outgoing, gate_up_b, down_b = lax.optimization_barrier((outgoing, gate_up_b, down_b))
    received = lax.all_to_all(
        outgoing.reshape(16, CAP * N_Z, 2048), ("grp", "y"), 0, 0, tiled=True
    )
    gate_up = jnp.concatenate([gate_up, gate_up_b], axis=2)
    down = jnp.concatenate([down, down_b], axis=0)
    result = ffn(received.reshape(slots, 2048), gate_up, down)
    returned = lax.all_to_all(
        result.reshape(16, CAP * N_Z, 2048), ("grp", "y"), 0, 0, tiled=True
    )
    moe_part, *firsts = combine(gate, returned.reshape(slots, 2048))
    moe = ring_scatter(moe_part.reshape(8, 64, 2048), firsts)
    return (middle_f + moe).astype(BF16)[None]


def solution(mesh):
    split = Mesh(mesh.devices.reshape(2, 4, 8, 4), ("role", "grp", "z", "y"))
    seq = ("z", "y")
    in_specs = (
        P(("role", "grp"), seq, None),
        P(("role", "grp"), None),
        P(("role", "grp"), seq, None),
        P(("role", "grp"), seq, None),
        P(),
        P(),
        P(),
        P(),
        P(None, seq),
        P(),
        P(seq, None),
        P(("grp", "z", "y"), None, None, "role"),
        P(("grp", "z", "y"), "role", None),
    )
    out_specs = P(("role", "grp"), seq, None)

    return jax.shard_map(body, mesh=split, in_specs=in_specs, out_specs=out_specs, check_vma=False)
```

```python
import math

import jax
import jax.numpy as jnp
from jax import lax
from jax.experimental import pallas as pl
from jax.experimental.pallas import tpu as pltpu
from jax.sharding import Mesh, PartitionSpec as P


NODE = 32
CAP = 6
EPSILON = 1e-06
ROPE_BASE = 1000000.0
MASKED = -1e30
BF16 = jnp.bfloat16
F32 = jnp.float32
N_Z = 8
N_Y = 4
CHUNK = 12
LISTED = 72
VMEM_LIMIT = 16 * 1024 * 1024
SPLIT_AHEAD = 896
SPLIT_BACK = 1280


def shift(x, axis, size, by):
    return lax.ppermute(x, axis, [(i, (i + by) % size) for i in range(size)])


def ring_gather(x):
    fwd, bwd = [x], [x]
    for step in range(4):
        fwd.append(shift(fwd[-1], "z", N_Z, 1))
        if step < 3:
            bwd.append(shift(bwd[-1], "z", N_Z, N_Z - 1))
    return fwd + bwd[:0:-1]


def ring_scatter(slabs, firsts):
    def plus(a, b):
        return (a.astype(F32) + b.astype(F32)).astype(BF16)

    def ahead(part, cols):
        for k in (5, 6, 7):
            part = plus(shift(part, "z", N_Z, 1), slabs[k, :, cols])
        return shift(part, "z", N_Z, 1)

    def back(part, cols):
        for k in (2, 1):
            part = plus(shift(part, "z", N_Z, N_Z - 1), slabs[k, :, cols])
        return shift(part, "z", N_Z, N_Z - 1)

    fwd = [ahead(firsts[0], slice(0, SPLIT_AHEAD)), ahead(firsts[1], slice(SPLIT_AHEAD, 2048))]
    bwd = [back(firsts[2], slice(0, SPLIT_BACK)), back(firsts[3], slice(SPLIT_BACK, 2048))]
    fwd, bwd = jnp.concatenate(fwd, axis=1), jnp.concatenate(bwd, axis=1)
    return fwd.astype(F32) + bwd.astype(F32) + slabs[0].astype(F32)


FIRST_SHAPES = tuple(
    jax.ShapeDtypeStruct((64, w), BF16)
    for w in (SPLIT_AHEAD, 2048 - SPLIT_AHEAD, SPLIT_BACK, 2048 - SPLIT_BACK)
)


def resident():
    return pl.BlockSpec(memory_space=pltpu.VMEM)


def rms_scale(values, gain):
    mean_sq = jnp.mean(values * values, axis=-1, keepdims=True)
    return values * lax.rsqrt(mean_sq + EPSILON) * gain


def kv_kernel(kv_ref, *refs):
    pieces_a, pieces_b = refs[:N_Z], refs[N_Z : 2 * N_Z]
    gain, wkv, cosd, sind, kg, kv_out, n_out, meta_out = refs[2 * N_Z :]
    width = pieces_a[0].shape[1]
    for k in range(N_Z):
        rows = slice(k * 64, (k + 1) * 64)
        fa = pieces_a[k][...].astype(F32)
        fb = pieces_b[k][:, :width].astype(F32)
        mean_sq = (
            jnp.sum(fa * fa, axis=-1, keepdims=True) + jnp.sum(fb * fb, axis=-1, keepdims=True)
        ) / (2 * width)
        scale = lax.rsqrt(mean_sq + EPSILON)
        n_out[rows, :width] = (fa * scale * gain[:, :width]).astype(BF16)
        n_out[rows, width:] = (fb * scale * gain[:, width:]).astype(BF16)
        meta_out[rows] = pieces_b[k][:, width:]
    proj = jnp.dot(n_out[...], wkv[0], preferred_element_type=F32).astype(BF16)
    u = rms_scale(proj[:, :128].astype(F32), kg[...])
    keys = (u * cosd[...] + pltpu.roll(u, 64, 1) * sind[...]).astype(BF16)
    for copy in range(N_Y):
        kv_out[copy, :, :128] = keys
        kv_out[copy, :, 128:] = proj[:, 128:]


def project_kv(kv_index, xa, xb, gain, w_keyval, cosd, sind, k_gain):
    total = 64 * N_Z
    whole = lambda shape: pl.BlockSpec(shape, lambda i, s: (0,) * len(shape))
    return pl.pallas_call(
        kv_kernel,
        out_shape=(
            jax.ShapeDtypeStruct((N_Y, total, 256), BF16),
            jax.ShapeDtypeStruct((total, 2048), BF16),
            jax.ShapeDtypeStruct((total, 128), BF16),
        ),
        grid_spec=pltpu.PrefetchScalarGridSpec(
            num_scalar_prefetch=1,
            grid=(1,),
            in_specs=[resident() for p in xa + xb]
            + [
                whole((1, 2048)),
                pl.BlockSpec((1, 2048, 256), lambda i, s: (s[0], 0, 0)),
                whole((total, 128)),
                whole((total, 128)),
                whole((1, 128)),
            ],
            out_specs=(
                whole((N_Y, total, 256)),
                whole((total, 2048)),
                whole((total, 128)),
            ),
        ),
        compiler_params=pltpu.CompilerParams(vmem_limit_bytes=VMEM_LIMIT),
        name="project_kv",
    )(kv_index, *xa, *xb, gain, w_keyval, cosd, sind, k_gain)


def q_kernel(n, wq0, wq1, wq2, wq3, cosd, sind, qg, q_out, w_scr):
    @pl.when(pl.program_id(0) == 0)
    def _():
        for h, w in enumerate((wq0, wq1, wq2, wq3)):
            w_scr[:, h * 128 : (h + 1) * 128] = w[...]

    proj = jnp.dot(n[...], w_scr[...], preferred_element_type=F32).astype(BF16)
    cos = cosd[...]
    sin = sind[...]
    for h in range(4):
        u = rms_scale(proj[:, h * 128 : (h + 1) * 128].astype(F32), qg[...])
        q_out[h] = (u * cos + pltpu.roll(u, 64, 1) * sin).astype(BF16)


def project_q(n, wq, cosd, sind, q_gain):
    rows = 256
    total = n.shape[0]
    whole = lambda shape: pl.BlockSpec(shape, lambda i: (0,) * len(shape))
    return pl.pallas_call(
        q_kernel,
        out_shape=jax.ShapeDtypeStruct((4, total, 128), BF16),
        grid=(total // rows,),
        in_specs=[pl.BlockSpec((rows, 2048), lambda i: (i, 0))]
        + [resident()] * 4
        + [
            pl.BlockSpec((rows, 128), lambda i: (i, 0)),
            pl.BlockSpec((rows, 128), lambda i: (i, 0)),
            whole((1, 128)),
        ],
        out_specs=pl.BlockSpec((4, rows, 128), lambda i: (0, i, 0)),
        scratch_shapes=[pltpu.VMEM((2048, 512), BF16)],
        compiler_params=pltpu.CompilerParams(vmem_limit_bytes=VMEM_LIMIT),
        name="project_q",
    )(n, *wq, cosd, sind, q_gain)


def attend_kernel(
    table, q, kv, seen, wo0, wo1, wo2, wo3, out, fa, fb, ba, bb, att, w_scr, kv_scr
):
    step_id = pl.program_id(0)
    z = table[0]
    keys = CHUNK * NODE

    @pl.when(step_id == 0)
    def _():
        for h, w in enumerate((wo0, wo1, wo2, wo3)):
            w_scr[h * 128 : (h + 1) * 128] = w[...]

    inv_scale = 1.0 / math.sqrt(128)
    row = lax.broadcasted_iota(jnp.int32, (64, keys), 0)
    col = lax.broadcasted_iota(jnp.int32, (64, keys), 1)
    later = (col < 64) & (row // NODE == col // NODE) & (col > row)
    bases = [8 + (2 * step_id + b) * (8 + LISTED) for b in range(2)]
    queries = [q[:, b * 64 : (b + 1) * 64].reshape(256, 128) for b in range(2)]

    def load(b, chunk):
        for s in range(CHUNK):
            node = table[bases[b] + 8 + chunk * CHUNK + s]
            plane = lax.rem(z - node // 8 + N_Z, N_Z)
            start = pl.multiple_of(plane * 64 + (node % 2) * NODE, NODE)
            kv_scr[b, s * NODE : (s + 1) * NODE] = kv[(node % 8) // 2, pl.ds(start, NODE), :]
        cols = pl.ds(pl.multiple_of(chunk * keys, keys), keys)
        mask = jnp.where(row < NODE, seen[b, 0:1, cols], seen[b, 1:2, cols]) < 0.5
        scores = (
            lax.dot_general(
                queries[b],
                kv_scr[b, :, :128],
                (((1,), (1,)), ((), ())),
                preferred_element_type=F32,
            )
            * inv_scale
        )
        return scores.reshape(4, 64, keys), mask

    def weighed(b, probs):
        return jnp.dot(probs.astype(BF16), kv_scr[b, :, 128:], preferred_element_type=F32)

    firsts = [load(b, 0) for b in range(2)]
    scores = [
        jnp.where((mask | later)[None], MASKED, sc).reshape(256, keys) for sc, mask in firsts
    ]
    tops = [jnp.max(sc, axis=-1, keepdims=True) for sc in scores]
    probs = [jnp.exp(sc - top) for sc, top in zip(scores, tops)]
    totals = [jnp.sum(p, axis=-1, keepdims=True) for p in probs]
    mixes = [weighed(b, probs[b]) for b in range(2)]

    for b in range(2):

        def step(chunk, carry, b=b):
            top, total, mixed = carry
            scores, mask = load(b, chunk)
            scores = jnp.where(mask[None], MASKED, scores).reshape(256, keys)
            new_top = jnp.maximum(top, jnp.max(scores, axis=-1, keepdims=True))
            old = jnp.exp(top - new_top)
            probs = jnp.exp(scores - new_top)
            total = old * total + jnp.sum(probs, axis=-1, keepdims=True)
            return new_top, total, old * mixed + weighed(b, probs)

        chunks = (table[bases[b]] + CHUNK - 1) // CHUNK
        _, total, mixed = lax.fori_loop(1, chunks, step, (tops[b], totals[b], mixes[b]))
        attended = (mixed / total).astype(BF16)
        at = pl.multiple_of((2 * step_id + b) * 64, 64)
        for h in range(4):
            att[pl.ds(at, 64), h * 128 : (h + 1) * 128] = attended[h * 64 : (h + 1) * 64]

    @pl.when(step_id == N_Z // 2 - 1)
    def _():
        full = jnp.dot(att[...], w_scr[...], preferred_element_type=F32).astype(BF16)
        out[...] = full
        fa[...] = full[256:320, :SPLIT_AHEAD]
        fb[...] = full[256:320, SPLIT_AHEAD:]
        ba[...] = full[192:256, :SPLIT_BACK]
        bb[...] = full[192:256, SPLIT_BACK:]


def attend(table, q, kv, seen, wo):
    whole = lambda shape: pl.BlockSpec(shape, lambda i, s: (0,) * len(shape))
    return pl.pallas_call(
        attend_kernel,
        out_shape=(jax.ShapeDtypeStruct((512, 2048), BF16),) + FIRST_SHAPES,
        grid_spec=pltpu.PrefetchScalarGridSpec(
            num_scalar_prefetch=1,
            grid=(N_Z // 2,),
            in_specs=[
                pl.BlockSpec((4, 128, 128), lambda i, s: (0, i, 0)),
                resident(),
                pl.BlockSpec((2, 2, LISTED * NODE), lambda i, s: (i, 0, 0)),
                resident(),
                resident(),
                resident(),
                resident(),
            ],
            out_specs=(whole((512, 2048)),) + tuple(whole(f.shape) for f in FIRST_SHAPES),
            scratch_shapes=[
                pltpu.VMEM((512, 512), BF16),
                pltpu.VMEM((512, 2048), BF16),
                pltpu.VMEM((2, CHUNK * NODE, 256), BF16),
            ],
        ),
        compiler_params=pltpu.CompilerParams(vmem_limit_bytes=VMEM_LIMIT),
        name="attend",
    )(table, q, kv, seen, *wo)


def route_kernel(place, meta, spread_out, gate_out):
    slots = spread_out.shape[0]
    rows = meta.shape[0]
    per = slots // 16
    z = place[0]
    info = meta[...].astype(F32)
    member = lax.broadcasted_iota(jnp.int32, (1, 128), 1)
    expert = (member // N_Y) * (N_Z * N_Y) + z * N_Y + member % N_Y
    expert = jnp.where(member < 16, expert, -1).astype(F32)
    hot = jnp.zeros((rows, 128), F32)
    high = jnp.zeros((rows, 128), F32)
    for i in range(8):
        same = info[:, i : i + 1] == expert
        hot = hot + jnp.where(same, 1.0, 0.0)
        high = high + jnp.where(same, info[:, 8 + i : 9 + i], 0.0)
    upto = lax.broadcasted_iota(jnp.int32, (rows, rows), 0) >= lax.broadcasted_iota(
        jnp.int32, (rows, rows), 1
    )
    count = jnp.dot(
        jnp.where(upto, 1.0, 0.0).astype(BF16), hot.astype(BF16), preferred_element_type=F32
    )
    rank = (count * hot).astype(BF16)
    slot_of = lax.broadcasted_iota(jnp.int32, (128, slots), 1) // per
    grow = jnp.where(
        slot_of == lax.broadcasted_iota(jnp.int32, (128, slots), 0), 1.0, 0.0
    ).astype(BF16)
    wide = jnp.dot(rank, grow, preferred_element_type=F32)
    nth = (lax.broadcasted_iota(jnp.int32, (1, slots), 1) % per + 1).astype(F32)
    at = wide == nth
    gate_out[...] = jnp.where(
        at, jnp.dot(high.astype(BF16), grow, preferred_element_type=F32), 0.0
    ).astype(BF16)
    spread_out[...] = jnp.where(at, 1.0, 0.0).T.astype(BF16)


def route(place, meta, slots):
    rows = meta.shape[0]
    whole = lambda shape: pl.BlockSpec(shape, lambda i, s: (0,) * len(shape))
    return pl.pallas_call(
        route_kernel,
        out_shape=(
            jax.ShapeDtypeStruct((slots, rows), BF16),
            jax.ShapeDtypeStruct((rows, slots), BF16),
        ),
        grid_spec=pltpu.PrefetchScalarGridSpec(
            num_scalar_prefetch=1,
            grid=(1,),
            in_specs=[whole(meta.shape)],
            out_specs=(whole((slots, rows)), whole((rows, slots))),
        ),
        compiler_params=pltpu.CompilerParams(vmem_limit_bytes=VMEM_LIMIT),
        name="route",
    )(place, meta)


def ffn_kernel(x, gate_up, down, out):
    rows = x[...]
    gate = jnp.dot(rows, gate_up[0], preferred_element_type=F32)
    up = jnp.dot(rows, gate_up[1], preferred_element_type=F32)
    hidden = (gate / (1.0 + jnp.exp(-gate)) * up).astype(BF16)
    out[...] = jnp.dot(hidden, down[...], preferred_element_type=F32).astype(BF16)


def ffn(x, gate_up, down):
    rows = 256
    width = x.shape[1]
    return pl.pallas_call(
        ffn_kernel,
        out_shape=jax.ShapeDtypeStruct(x.shape, BF16),
        grid=(x.shape[0] // rows,),
        in_specs=[pl.BlockSpec((rows, width), lambda i: (i, 0)), resident(), resident()],
        out_specs=pl.BlockSpec((rows, width), lambda i: (i, 0)),
        compiler_params=pltpu.CompilerParams(vmem_limit_bytes=VMEM_LIMIT),
        name="ffn",
    )(x, gate_up, down)


def spread_kernel(*refs):
    pieces_a, pieces_b = refs[:N_Z], refs[N_Z : 2 * N_Z]
    spread, out, rows = refs[2 * N_Z :]
    width = pieces_a[0].shape[1]

    @pl.when(pl.program_id(0) == 0)
    def _():
        for k in range(N_Z):
            rows[k * 64 : (k + 1) * 64, :width] = pieces_a[k][...]
            rows[k * 64 : (k + 1) * 64, width:] = pieces_b[k][...]

    out[...] = jnp.dot(spread[...], rows[...], preferred_element_type=F32).astype(BF16)


def spread_rows(spread, pa, pb):
    width = 2 * pa[0].shape[1]
    slots, tokens = spread.shape
    return pl.pallas_call(
        spread_kernel,
        out_shape=jax.ShapeDtypeStruct((slots, width), BF16),
        grid=(slots // 256,),
        in_specs=[resident() for p in pa + pb]
        + [pl.BlockSpec((256, tokens), lambda i: (i, 0))],
        out_specs=pl.BlockSpec((256, width), lambda i: (i, 0)),
        scratch_shapes=[pltpu.VMEM((tokens, width), BF16)],
        compiler_params=pltpu.CompilerParams(vmem_limit_bytes=VMEM_LIMIT),
        name="spread",
    )(*pa, *pb, spread)


def combine_kernel(g, r, out, fa, fb, ba, bb):
    full = jnp.dot(g[...], r[...], preferred_element_type=F32).astype(BF16)
    out[...] = full

    @pl.when(pl.program_id(0) == 0)
    def _():
        ba[...] = full[192:256, :SPLIT_BACK]
        bb[...] = full[192:256, SPLIT_BACK:]

    @pl.when(pl.program_id(0) == 1)
    def _():
        fa[...] = full[:64, :SPLIT_AHEAD]
        fb[...] = full[:64, SPLIT_AHEAD:]


def combine(g, r):
    rows = 256
    return pl.pallas_call(
        combine_kernel,
        out_shape=(jax.ShapeDtypeStruct((g.shape[0], r.shape[1]), BF16),) + FIRST_SHAPES,
        grid=(g.shape[0] // rows,),
        in_specs=[pl.BlockSpec((rows, g.shape[1]), lambda i: (i, 0)), resident()],
        out_specs=(pl.BlockSpec((rows, r.shape[1]), lambda i: (i, 0)),)
        + tuple(pl.BlockSpec(f.shape, lambda i: (0, 0)) for f in FIRST_SHAPES),
        compiler_params=pltpu.CompilerParams(vmem_limit_bytes=VMEM_LIMIT),
        name="combine",
    )(g, r)


def ancestry(parent_row):
    nodes = parent_row.shape[0]
    ids = jnp.arange(nodes, dtype=jnp.int32)
    reach = ((parent_row[:, None] == ids[None, :]) | (ids[:, None] == ids[None, :])).astype(BF16)
    for _ in range((nodes - 1).bit_length()):
        reach = (jnp.dot(reach, reach, preferred_element_type=F32) > 0.5).astype(BF16)
    return reach


def body(
    tokens,
    parents,
    route_ids,
    route_gates,
    input_gain,
    q_gain,
    k_gain,
    post_gain,
    w_query,
    w_keyval,
    w_out,
    w_gate_up,
    w_down,
):
    z = lax.axis_index("z")
    y = lax.axis_index("y")
    place = jnp.stack([z, y]).astype(jnp.int32)
    half = 1024
    swap = [(0, 1), (1, 0)]

    meta = jnp.concatenate(
        [route_ids[0].astype(BF16), route_gates[0].astype(BF16), jnp.zeros((64, 112), BF16)], axis=1
    )
    own = tokens[0]
    xa = ring_gather(own[:, :half])
    xb = ring_gather(jnp.concatenate([own[:, half:], meta], axis=1))
    wq = [w_query] + [shift(w_query, "y", N_Y, k) for k in (1, 3, 2)]
    wo = [w_out] + [shift(w_out, "y", N_Y, k) for k in (1, 3, 2)]

    reach = ancestry(parents[0])
    depth = jnp.sum(reach.astype(F32), axis=1) - 1.0
    node_ids = jnp.arange(64, dtype=jnp.int32)
    t512 = jnp.arange(512, dtype=jnp.int32)
    node_of = ((z - t512 // 64) % N_Z) * 8 + y * 2 + (t512 % 64) // NODE
    depth_of = jnp.sum(
        jnp.where(node_of[:, None] == node_ids[None, :], depth[None, :], 0.0), axis=1
    )
    positions = depth_of * NODE + (t512 % NODE).astype(F32)
    frequency = jnp.power(ROPE_BASE, -2.0 * jnp.arange(64, dtype=F32) / 128)
    angles = positions[:, None] * frequency[None, :]
    cosine = jnp.cos(angles)
    sine = jnp.sin(angles)
    cosd = jnp.concatenate([cosine, cosine], axis=1)
    sind = jnp.concatenate([-sine, sine], axis=1)

    first = ((z - jnp.arange(8, dtype=jnp.int32)) % N_Z) * 8 + y * 2
    is_a = (first[:, None] == node_ids[None, :]).astype(BF16)
    is_b = (first[:, None] + 1 == node_ids[None, :]).astype(BF16)
    see_a = jnp.dot(is_a, reach, preferred_element_type=F32)
    see_b = jnp.dot(is_b, reach, preferred_element_type=F32)
    own_two = (is_a + is_b).astype(F32)
    others = jnp.where(own_two > 0.5, 0.0, jnp.maximum(see_a, see_b))
    before = (node_ids[:, None] < node_ids[None, :]).astype(BF16)
    rank = jnp.dot(others.astype(BF16), before, preferred_element_type=F32) + 2.0
    at = jnp.where(others > 0.5, rank, jnp.where(own_two > 0.5, is_b.astype(F32), -1.0))
    spots = jnp.arange(LISTED, dtype=jnp.int32)
    listed = (at[:, :, None] == spots.astype(F32)[None, None, :]).astype(F32)
    nodes = jnp.sum(listed * node_ids.astype(F32)[None, :, None], axis=1).astype(jnp.int32)
    count = jnp.sum(others, axis=1).astype(jnp.int32) + 2
    table = jnp.concatenate(
        [jnp.broadcast_to(count[:, None], (8, 8)), nodes], axis=1
    ).reshape(-1)
    table = jnp.concatenate([jnp.broadcast_to(z, (8,)).astype(jnp.int32), table])
    vis = jnp.stack(
        [jnp.sum(listed * see_a[:, :, None], axis=1), jnp.sum(listed * see_b[:, :, None], axis=1)],
        axis=1,
    ).reshape(16, LISTED)
    wide = jnp.arange(LISTED * NODE, dtype=jnp.int32)
    grow = (spots[:, None] == wide[None, :] // NODE).astype(BF16)
    seen = jnp.dot(vis.astype(BF16), grow, preferred_element_type=F32)
    seen = seen.reshape(8, 2, LISTED * NODE)

    cosd, sind, table, seen = lax.optimization_barrier((cosd, sind, table, seen))
    kv, normed, meta_col = project_kv(
        (z // 2).reshape(1).astype(jnp.int32),
        xa,
        xb,
        input_gain.reshape(1, -1),
        w_keyval,
        cosd,
        sind,
        k_gain.reshape(1, -1),
    )
    kv_all = lax.all_to_all(kv, "y", 0, 0, tiled=True)
    q = project_q(normed, wq, cosd, sind, q_gain.reshape(1, -1))
    slots = 16 * CAP * N_Z
    spread, gate = route(place, meta_col, slots)
    kv_all, spread, gate = lax.optimization_barrier((kv_all, spread, gate))
    partial, *firsts = attend(table, q, kv_all, seen, wo)
    attn = ring_scatter(partial.reshape(8, 64, 2048), firsts)
    middle = (own.astype(F32) + attn).astype(BF16)
    middle_f = middle.astype(F32)
    post_normed = rms_scale(middle_f, post_gain).astype(BF16)

    pa = ring_gather(post_normed[:, :half])
    pb = ring_gather(post_normed[:, half:])
    outgoing = spread_rows(spread, pa, pb)
    outgoing, gate_up, down = lax.optimization_barrier((outgoing, w_gate_up[0], w_down[0]))
    received = lax.all_to_all(outgoing.reshape(16, CAP * N_Z, 2048), ("grp", "y"), 0, 0, tiled=True)
    gate_up_b = lax.ppermute(gate_up, "role", swap)
    down_b = lax.ppermute(down, "role", swap)
    gate_up = jnp.concatenate([gate_up, gate_up_b], axis=2)
    down = jnp.concatenate([down, down_b], axis=0)
    result = ffn(received.reshape(slots, 2048), gate_up, down)
    returned = lax.all_to_all(
        result.reshape(16, CAP * N_Z, 2048), ("grp", "y"), 0, 0, tiled=True
    )
    moe_part, *firsts = combine(gate, returned.reshape(slots, 2048))
    moe = ring_scatter(moe_part.reshape(8, 64, 2048), firsts)
    return (middle_f + moe).astype(BF16)[None]


def solution(mesh):
    split = Mesh(mesh.devices.reshape(2, 4, 8, 4), ("role", "grp", "z", "y"))
    seq = ("z", "y")
    in_specs = (
        P(("role", "grp"), seq, None),
        P(("role", "grp"), None),
        P(("role", "grp"), seq, None),
        P(("role", "grp"), seq, None),
        P(),
        P(),
        P(),
        P(),
        P(None, seq),
        P(),
        P(seq, None),
        P(("grp", "z", "y"), None, None, "role"),
        P(("grp", "z", "y"), "role", None),
    )
    out_specs = P(("role", "grp"), seq, None)

    return jax.shard_map(body, mesh=split, in_specs=in_specs, out_specs=out_specs, check_vma=False)
```
